32 devices in a mesh: groups: 2 (over y), shot: 4 (over z), depth: 2 (over x), freq: 2 (over core).
Axes of the slice: x: 2, y: 2, z: 4, core: 2. Of those that a mesh axis runs over, the one named last changes fastest.
Arguments:
- source: float32 [8, 6, 2, 256, 256], P(('groups', 'shot'), 'freq'), parts along dimension 0, may hold values from -6 to 6
- receiver: float32 [8, 6, 2, 256, 256], P(('groups', 'shot'), 'freq'), parts along dimension 0, may hold values from -6 to 6
- slowness: float32 [8, 4, 256, 256], P(('groups', 'shot'), 'depth'), parts along dimension 0, may hold values from 0.6 to 1.4
- omegas: float32 [8, 6], P(('groups', 'shot'), 'freq'), parts along dimension 0, may hold values from 0.5 to 2.5
- shot_start: int32 [8], P(('groups', 'shot')), parts along dimension 0, may hold values from 0 to 256, as said below
Outputs:
- image: float32 [1024, 4, 256], P(('groups', 'shot'), 'depth', 'freq'), parts along dimension 0
The draws below stay inside these ranges and needn't reach their ends.
There are 2 independent parts, one for each index of `groups`. The reference program is written for one: setup_inputs(seed, part) draws one part's arguments, and reference() takes and returns one part's arrays. A program takes and returns all parts, laid end to end along the dimension named above; each array names one. Nothing has to cross between parts.
Inputs may be any that keep to these rules, and one draw needn't show every extreme that they name: `shot_start`: any shot group's aperture may begin at any column of the survey. Shot group 4 // 2 begins at column 0 and shot group 0 at 256.
All inputs are finite; a program needn't handle non-finite values.
Results may differ from the reference program's by a relative error of at most 0.03.
Values may be sent and summed in bfloat16 or wider, within the bound.
No kernel may reach another device: no remote copies, remote signals or barrier semaphores. Data moves between devices by JAX's collectives and lax.ppermute only.
A program may use at most 64 MiB of HBM per device.

```python
import math
import jax
import jax.numpy as jnp
from jax import lax

AP = 256
FRONTS = 6
NSHOTS = 4
NZ = 4
IMG_X = 512


def draw_shot_start(key, part):
    positions = jnp.arange(NSHOTS, dtype=jnp.int32)
    begins = jax.random.randint(jax.random.fold_in(key, 11), (NSHOTS,), 0, IMG_X - AP + 1, dtype=jnp.int32)
    begins = jnp.where(positions == NSHOTS // 2, 0, begins)
    begins = jnp.where(positions == 0, IMG_X - AP, begins)
    return begins.astype(jnp.int32)


def block_scale(stream_key, extent, shards, smallest, high):
    def one(position, shards_of):
        draws = jax.random.uniform(jax.random.fold_in(jax.random.fold_in(stream_key, 6), position), (shards_of,), jnp.float32, smallest / len(shards), high / len(shards))
        return jnp.repeat(jnp.exp(draws), extent[position] // shards_of).reshape((-1,) + (1,) * (len(extent) - position - 1))

    level = one(*shards[0])
    for cut in shards[1:]:
        level = level * one(*cut)
    return level


def normal_values(rng, shape, deviation, reach, cuts=(), held_as=jnp.bfloat16):
    values = jax.random.normal(rng, shape, jnp.float32) * deviation
    if len(cuts) > 0:
        values = block_scale(rng, shape, cuts, -0.22, 0.18) * values
    return jnp.clip(values, min=-reach, max=reach).astype(held_as)


def setup_inputs(seed: int = 0, part: int = 0) -> dict:
    arg_keys = jax.random.split(jax.random.key(seed), 6)
    part_keys = jax.random.split(jax.random.fold_in(arg_keys[5], part), 6)
    source = normal_values(part_keys[0], (NSHOTS, FRONTS, 2, AP, AP), 1.0, 6.0, ((0, 4), (1, 2)), jnp.float32)
    receiver = normal_values(part_keys[1], (NSHOTS, FRONTS, 2, AP, AP), 1.0, 6.0, ((0, 4), (1, 2)), jnp.float32)
    slowness = jnp.clip(jnp.exp(math.log(1.4) - 0.8472978 * jax.random.uniform(part_keys[2], (NSHOTS, NZ, AP, AP), jnp.float32) ** block_scale(part_keys[2], (NSHOTS, NZ, AP, AP), ((0, 4), (1, 2)), -0.2, 0.2)), 0.6, 1.4)
    omegas = jnp.clip(jnp.exp(math.log(2.5) - 1.609438 * jax.random.uniform(part_keys[3], (NSHOTS, FRONTS), jnp.float32) ** block_scale(part_keys[3], (NSHOTS, FRONTS), ((0, 4), (1, 2)), -0.2, 0.2)), 0.5, 2.5)
    shot_start = draw_shot_start(jax.random.fold_in(jax.random.fold_in(arg_keys[5], part), 71), part)
    return dict(source=source, receiver=receiver, slowness=slowness, omegas=omegas, shot_start=shot_start)


def tables(points):
    positions = jnp.arange(points, dtype=jnp.int32)
    product = positions[:, None] * positions[None, :] % points
    angles = 2.0 * jnp.pi / points * product.astype(jnp.float32)
    cosine_table = jnp.cos(angles).astype(jnp.bfloat16)
    sine_table = jnp.sin(angles).astype(jnp.bfloat16)
    forward = jnp.concatenate([jnp.concatenate([cosine_table, -sine_table], axis=1), jnp.concatenate([sine_table, cosine_table], axis=1)], axis=0)
    inverse = jnp.concatenate([jnp.concatenate([cosine_table, sine_table], axis=1), jnp.concatenate([-sine_table, cosine_table], axis=1)], axis=0)
    return (forward, inverse)

def lateral_grids(points):
    positions = jnp.arange(points, dtype=jnp.int32)
    wrapped = (positions + points // 2) % points - points // 2
    wavenumber = 2.0 * jnp.pi / points * wrapped.astype(jnp.float32)
    edge_width = points // 16
    distance_in = jnp.minimum(positions, points - 1 - positions) + 1
    edge_taper = jnp.minimum(distance_in.astype(jnp.float32) / edge_width, 1.0)
    return (wavenumber, edge_taper)

def flip_parts(field_in):
    leading = field_in.shape[:-2]
    row_count = field_in.shape[-2]
    col_count = field_in.shape[-1] // 2
    pieces = field_in.reshape(leading + (row_count, 2, col_count))
    moved = jnp.swapaxes(pieces, -3, -1)
    return moved.reshape(leading + (col_count, 2 * row_count))

def extrapolate(wave_state, slow_level, angular, field_signs, forward, inverse, wavenumber, edge_taper):
    batch_size, points, width = wave_state.shape
    inv_points = 1.0 / points
    half_done = jnp.dot(wave_state.reshape(batch_size * points, width), forward, preferred_element_type=jnp.float32)
    half_done = flip_parts(half_done.astype(jnp.bfloat16).reshape(batch_size, points, width))
    spectrum = jnp.dot(half_done.reshape(batch_size * points, width), forward, preferred_element_type=jnp.float32).reshape(batch_size, points, width)
    mean_slow = jnp.mean(slow_level)
    radius_sq = jnp.square(angular * mean_slow)
    square = jnp.square(wavenumber)[:, None] + jnp.square(wavenumber)[None, :]
    vertical = radius_sq[:, None, None] - square[None]
    real_kz = jnp.sqrt(jnp.maximum(vertical, 0.0))
    damping = jnp.exp(-jnp.sqrt(jnp.maximum(-vertical, 0.0)))
    phase_turn = field_signs[:, None, None] * real_kz
    phase_real = damping * jnp.cos(phase_turn)
    phase_imag = damping * jnp.sin(phase_turn)
    spec_real = spectrum[..., :points]
    spec_imag = spectrum[..., points:]
    shifted = jnp.concatenate([spec_real * phase_real - spec_imag * phase_imag, spec_real * phase_imag + spec_imag * phase_real], axis=-1).astype(jnp.bfloat16)
    half_back = jnp.dot(shifted.reshape(batch_size * points, width), inverse, preferred_element_type=jnp.float32) * inv_points
    half_back = flip_parts(half_back.astype(jnp.bfloat16).reshape(batch_size, points, width))
    field_out = jnp.dot(half_back.reshape(batch_size * points, width), inverse, preferred_element_type=jnp.float32).reshape(batch_size, points, width) * inv_points
    correction = (field_signs * angular)[:, None, None] * (slow_level - mean_slow)[None]
    window = edge_taper[:, None] * edge_taper[None, :]
    corr_real = jnp.cos(correction) * window[None]
    corr_imag = jnp.sin(correction) * window[None]
    field_real = field_out[..., :points]
    field_imag = field_out[..., points:]
    return (field_real * corr_real - field_imag * corr_imag, field_real * corr_imag + field_imag * corr_real)

def reference(source, receiver, slowness, omegas, shot_start):
    points = source.shape[-1]
    fronts = source.shape[1]
    forward, inverse = tables(points)
    wavenumber, edge_taper = lateral_grids(points)
    field_signs = jnp.tile(jnp.array([-1.0, 1.0], jnp.float32), fronts)

    def one_shot(image_sum, shot_data):
        src_shot, rcv_shot, slow_shot, rate_shot, begin = shot_data
        paired = jnp.stack([src_shot, rcv_shot], axis=1)
        joined = jnp.concatenate([paired[:, :, 0], paired[:, :, 1]], axis=-1)
        wave_state = joined.reshape(fronts * 2, points, 2 * points).astype(jnp.bfloat16)
        angular = jnp.repeat(rate_shot, 2)

        def one_level(level_state, slow_level):
            real_part, imag_part = extrapolate(level_state, slow_level, angular, field_signs, forward, inverse, wavenumber, edge_taper)
            real_pair = real_part.reshape(fronts, 2, points, points)
            imag_pair = imag_part.reshape(fronts, 2, points, points)
            level_term = lax.optimization_barrier(jnp.sum(real_pair[:, 0] * real_pair[:, 1] + imag_pair[:, 0] * imag_pair[:, 1], axis=0))
            new_state = jnp.concatenate([real_part, imag_part], axis=-1).astype(jnp.bfloat16)
            return (new_state, level_term)
        final_state, level_terms = lax.scan(one_level, wave_state, slow_shot)
        placed = jnp.transpose(level_terms, (1, 0, 2))
        begin_row = begin.astype(jnp.int32)
        zero_index = jnp.zeros((), jnp.int32)
        current = lax.dynamic_slice(image_sum, (begin_row, zero_index, zero_index), placed.shape)
        image_sum = lax.dynamic_update_slice(image_sum, current + placed, (begin_row, zero_index, zero_index))
        return (image_sum, zero_index)
    initial = jnp.zeros((IMG_X, NZ, points), jnp.float32)
    image_sum, unused_out = lax.scan(one_shot, initial, (source, receiver, slowness, omegas, shot_start))
    return image_sum
```

```python
import functools

import jax
import jax.numpy as jnp
import ml_dtypes
import numpy as np
from jax import lax
from jax.experimental import pallas as pl
from jax.experimental.pallas import tpu as pltpu
from jax.sharding import PartitionSpec as P_

TILE = 128

def _fit(f, hi, deg):
    k = np.arange(400)
    x = (np.cos(np.pi * (k + 0.5) / 400) + 1) / 2 * hi
    c = np.polynomial.chebyshev.Chebyshev.fit(x, f(x), deg, domain=[0, hi])
    return [float(v) for v in c.convert(kind=np.polynomial.Polynomial).coef]
def _cosr(a): return np.cos(np.sqrt(a))
def _sinr(a): return np.sinc(np.sqrt(a) / np.pi)
PC = _fit(_cosr, 12.5, 6); PS = _fit(_sinr, 12.5, 5)
CC = _fit(_cosr, 4.1, 5); CS = _fit(_sinr, 4.1, 4)

def horner(co, x):
    r = co[-1] * x + co[-2]
    for c in co[-3::-1]:
        r = r * x + c
    return r

def make_tables(n):
    h, g = n // 2, n // 4
    idx = np.arange(n)
    ang = 2 * np.pi / n * (np.outer(idx, idx) % n)
    C = np.cos(ang).astype(ml_dtypes.bfloat16).astype(np.float32)
    S = np.sin(ang).astype(ml_dtypes.bfloat16).astype(np.float32)
    i = np.arange(g)
    ev = np.concatenate([2 * i, np.where(i == 0, h, n - 2 * i)])
    od = np.concatenate([2 * i + 1, n - 2 * i - 1])
    out = []
    for k in (ev, od):
        c, s = C[:h][:, k], S[:h][:, k]
        F = np.block([[c, -s], [s, c]])
        L = np.block([[c.T, s.T], [-s.T, c.T]])
        out.append((F, L, F / 1.0, L))
    T = []
    for p in (0, 1):
        k = (ev, od)[p]
        c, s = C[:h][:, k], S[:h][:, k]
        T.append(np.stack([np.block([[c, -s], [s, c]]), np.block([[c.T, s.T], [-s.T, c.T]]),
                           np.block([[c, -s], [s, c]]) / n, np.block([[c.T, s.T], [-s.T, c.T]]) / n]))
    T = np.stack(T, axis=1).astype(ml_dtypes.bfloat16)
    w = ((idx + h) % n - h).astype(np.float32)
    kk = (np.float32(2 * np.pi) / np.float32(n) * w).astype(np.float32)
    k2 = (kk * kk).astype(np.float32)
    base = np.concatenate([k2[2 * i], k2[2 * i + 1]])
    rows = np.concatenate([base, k2[h:h + 1]])
    K2 = np.zeros((h + 8, h), np.float32)
    K2[:h + 1] = rows[:, None] + base[None, :]
    K2[h + 1] = k2[h] + k2[h]
    ed = np.minimum(np.minimum(idx, n - 1 - idx) + 1, n // 16).astype(np.float32) / np.float32(n // 16)
    win = (ed[:, None] * ed[None, :]).astype(np.float32)
    return T, K2, win

def level_prep(n, s, win, D):
    s0 = jnp.sum(s[...]) * (1.0 / (n * n))
    d = s[...] - s0
    D[0] = d * d
    D[1] = d * win[...]
    return s0

def propagator(n, w2, K2, P):
    h, g = n // 2, n // 4
    a = w2 - K2[...]
    pos = a >= 0.0
    r = jnp.sqrt(jnp.abs(a))
    vals = (jnp.where(pos, horner(PC, a), jnp.exp(-r)), jnp.where(pos, r * horner(PS, a), 0.0))
    lane = lax.broadcasted_iota(jnp.int32, (8, h), 1)
    low, mid = lane < g, lane == g
    row0 = lax.broadcasted_iota(jnp.int32, (8, n), 0) == 0
    for comp in (0, 1):
        v = vals[comp]
        col = jnp.broadcast_to(v[h:h + 1], (h, h)).T
        for t in range(h // 8 + 1):
            p = v[8 * t:8 * t + 8]
            q = pltpu.roll(p, g, 1)
            cc = col[8 * t:8 * t + 8] if t < h // 8 else jnp.broadcast_to(v[h + 1:h + 2, :], (8, h))
            e = jnp.where(mid, cc, jnp.where(low, p, q))
            o = jnp.where(low, q, p)
            if t < g // 8:
                P[comp, 8 * t:8 * t + 8, :h] = e
                P[comp, 8 * t:8 * t + 8, h:] = o
                if t == 0:
                    e0, o0 = e, o
            elif t < h // 8:
                P[comp, 8 * t + 8:8 * t + 16, :h] = e
                P[comp, 8 * t + 8:8 * t + 16, h:] = o
            else:
                P[comp, g:g + 8, :h] = jnp.where(row0[:, :h], e, e0)
                P[comp, g:g + 8, h:] = jnp.where(row0[:, :h], o, o0)

def p_rows(n, P, comp, par):
    h, g = n // 2, n // 4
    if par == 0:
        return jnp.concatenate([P[comp, 0:g], P[comp, g:g + 8], P[comp, 8:g]], axis=0)
    o = P[comp, g + 8:h + 8]
    return jnp.concatenate([o, o], axis=0)

def corr(n, om, win, D, c):
    o2 = om * om
    cc, cs, f = [], [], jnp.float32(1.0)
    for k in range(max(len(CC), len(CS))):
        if k < len(CC): cc.append(CC[k] * f)
        if k < len(CS): cs.append(CS[k] * f * om)
        f = f * o2
    x = D[0]
    c[0] = win[...] * horner(cc, x)
    c[1] = D[1] * horner(cs, x)

def front_math(n, om, s0, T, K2, win, st, part, P, c, D):
    h = n // 2
    f32, bf = jnp.float32, jnp.bfloat16
    dot = functools.partial(jnp.dot, preferred_element_type=f32)
    w2 = om * s0; w2 = w2 * w2
    FL = ((0, -1.0), (1, 1.0))
    add, sub = (lambda a, b: a + b), (lambda a, b: a - b)
    def stack2(X, Y, op):
        re = jnp.concatenate([op(X[:h, :h], X[h:, :h]), op(Y[:h, :h], Y[h:, :h])], axis=1)
        im = jnp.concatenate([op(X[:h, h:], X[h:, h:]), op(Y[:h, h:], Y[h:, h:])], axis=1)
        return jnp.concatenate([re, im], axis=0).astype(bf)
    R = []
    for f, sg in FL:
        Ve = dot(st[f, 0], T[0, 0]); Vo = dot(st[f, 1], T[0, 1])
        R.append((stack2(Ve, Vo, add), stack2(Ve, Vo, sub)))
    propagator(n, w2, K2, P)
    W2 = []
    for f, sg in FL:
        out = []
        for p in (0, 1):
            W = dot(T[1, p], R[f][p])
            wr, wi = W[:h], W[h:]
            pr, pi = p_rows(n, P, 0, p), p_rows(n, P, 1, p)
            if sg > 0:
                out.append(jnp.concatenate([wr * pr - wi * pi, wr * pi + wi * pr], axis=0).astype(bf))
            else:
                out.append(jnp.concatenate([wr * pr + wi * pi, wi * pr - wr * pi], axis=0).astype(bf))
        W2.append(out)
    corr(n, om, win, D, c)
    YY = []
    for f, sg in FL:
        E = dot(T[2, 0], W2[f][0]); O = dot(T[2, 1], W2[f][1])
        U, Dn = E + O, E - O
        out = []
        for p in (0, 1):
            sl = slice(p * h, (p + 1) * h)
            out.append(jnp.concatenate([jnp.concatenate([U[:h, sl], U[h:, sl]], axis=1),
                                        jnp.concatenate([Dn[:h, sl], Dn[h:, sl]], axis=1)], axis=0).astype(bf))
        YY.append(out)
    res = []
    for f, sg in FL:
        Q0, Q1 = dot(YY[f][0], T[3, 0]), dot(YY[f][1], T[3, 1])
        X, Z = Q0 + Q1, Q0 - Q1
        halves = []
        for hf, q in ((0, X), (1, Z)):
            qr, qi = q[:, :h], q[:, h:]
            cr, ci = c[0, :, hf * h:(hf + 1) * h], c[1, :, hf * h:(hf + 1) * h]
            if sg > 0:
                halves.append((qr * cr - qi * ci, qr * ci + qi * cr))
            else:
                halves.append((qr * cr + qi * ci, qi * cr - qr * ci))
        (r0, i0), (r1, i1) = halves
        st[f, 0] = jnp.concatenate([r0 + r1, i0 + i1], axis=1).astype(bf)
        st[f, 1] = jnp.concatenate([r0 - r1, i0 - i1], axis=1).astype(bf)
        res.append(halves)
    for hf in (0, 1):
        (ur, ui), (wr, wi) = res[0][hf], res[1][hf]
        sl = slice(hf * h, (hf + 1) * h)
        part[:, sl] = part[:, sl] + (ur * wr + ui * wi)

def prep(n, src, st_ab):
    h = n // 2
    bf = jnp.bfloat16
    st_ab[0] = jnp.concatenate([src[0, :, :h] + src[0, :, h:], src[1, :, :h] + src[1, :, h:]], axis=1).astype(bf)
    st_ab[1] = jnp.concatenate([src[0, :, :h] - src[0, :, h:], src[1, :, :h] - src[1, :, h:]], axis=1).astype(bf)


ANY = pl.BlockSpec(memory_space=pl.ANY)
VM = pl.BlockSpec(memory_space=pltpu.VMEM)
SM = pl.BlockSpec(memory_space=pltpu.SMEM)
F32, BF16 = jnp.float32, jnp.bfloat16


def params(mib):
    return pltpu.CompilerParams(vmem_limit_bytes=mib * 1024 * 1024)


def first_levels(dims, who, om, src, rcv, slow, T, K2, win, st_out, own_out, raw, st, P, c, D, sem_in, sem_out):
    n, slots, L = dims
    nf, f0, levels = who[0], who[1], who[2]

    def moves(j):
        fr = f0 + j
        return (
            pltpu.make_async_copy(src.at[fr], raw.at[j, 0], sem_in.at[j, 0]),
            pltpu.make_async_copy(rcv.at[fr], raw.at[j, 1], sem_in.at[j, 1]),
        )

    for j in range(slots):
        @pl.when(j < nf)
        def _(j=j):
            for m in moves(j):
                m.start()
    for j in range(slots):
        @pl.when(j < nf)
        def _(j=j):
            for f, m in enumerate(moves(j)):
                m.wait()
                prep(n, raw.at[j, f], st.at[j, f])

    def level(z, _):
        s0 = level_prep(n, slow.at[z], win, D)
        own_out[z] = jnp.zeros((n, n), F32)

        def front(j, _):
            front_math(n, om[f0 + j], s0, T, K2, win, st.at[j], own_out.at[z], P, c, D)
            return 0

        lax.fori_loop(0, nf, front, 0)
        return 0

    lax.fori_loop(0, levels, level, 0)
    out = pltpu.make_async_copy(st, st_out, sem_out)
    out.start()
    out.wait()


def other_levels(dims, who, om, st_in, slow, got, own_in, T, K2, win, keep_own, send_own, keep_oth, send_oth,
                 st, s_now, part, P, c, D, sem):
    n, L, depth, freq = dims
    nf, f0, lo, d, fq = who[0], who[1], who[2], who[3], who[4]
    w = n // freq
    move = pltpu.make_async_copy(st_in, st, sem)
    move.start()

    def split(ref, keep, sends):
        for a in range(freq):
            @pl.when(fq == a)
            def _():
                keep[...] = ref[:, a * w:(a + 1) * w]
                for r in range(1, freq):
                    b = (a + r) % freq
                    sends.at[r - 1][...] = ref[:, b * w:(b + 1) * w].astype(BF16)

    @pl.when(lo > 0)
    def _():
        for z in range(L):
            split(own_in.at[z], keep_own.at[z], send_own.at[:, z])

    move.wait()

    def level(z, _):
        owner = z // L
        zl = z - owner * L
        back = lax.rem(d - owner + depth, depth)

        @pl.when(back == 0)
        def _():
            s_now[...] = slow[zl]

        @pl.when(back > 0)
        def _():
            s_now[...] = got[jnp.maximum(back - 1, 0), zl].astype(F32) + 1.0

        s0 = level_prep(n, s_now, win, D)
        part[...] = jnp.zeros((n, n), F32)

        def front(j, _):
            front_math(n, om[f0 + j], s0, T, K2, win, st.at[j], part, P, c, D)
            return 0

        lax.fori_loop(0, nf, front, 0)

        @pl.when(back == 0)
        def _():
            split(part, keep_own.at[zl], send_own.at[:, zl])

        @pl.when(back > 0)
        def _():
            r = jnp.maximum(depth - back - 1, 0)
            split(part, keep_oth.at[r, zl], send_oth.at[:, r, zl])

        return 0

    lax.fori_loop(lo, depth * L, level, 0)


def place(dims, where, own, got, out, padded):
    n, L, shots, more = dims
    w = own.shape[-1]
    survey = shots * TILE
    me, begin = where[0], where[1]
    padded[:, :survey] = jnp.zeros((L, survey, w), F32)
    padded[:, survey + n:] = jnp.zeros((L, survey, w), F32)
    for z in range(L):
        total = own[z]
        for r in range(more):
            total = total + got[r, z].astype(F32)
        padded[z, survey:survey + n] = total
    for r in range(shots):
        owner = lax.rem(me + r, shots)
        offset = jnp.clip(owner * TILE - begin + survey, 0, n + survey)
        for z in range(L):
            out[r, z] = padded[z, pl.ds(offset, TILE), :].astype(BF16)


def gather(dims, *refs):
    L, shots = dims
    out = refs[-1]
    for z in range(L):
        total = refs[0][z].astype(F32)
        for r in range(1, shots):
            total = total + refs[r][z].astype(F32)
        out[:, z, :] = total


def shift(array, axis, by):
    size = lax.axis_size(axis)
    return lax.ppermute(array, axis, [(i, (i + by) % size) for i in range(size)])


def local(source, receiver, slowness, omegas, shot_start):
    n = source.shape[-1]
    h = n // 2
    fronts, L = source.shape[1], slowness.shape[1]
    depth, freq, shots = lax.axis_size("depth"), lax.axis_size("freq"), lax.axis_size("shot")
    d, fq, me = lax.axis_index("depth"), lax.axis_index("freq"), lax.axis_index("shot")
    T, K2, win = make_tables(n)
    slots = -(-fronts // depth)
    base, extra = fronts // depth, fronts % depth
    nf = base + jnp.where(d < extra, 1, 0)
    f0 = d * base + jnp.minimum(d, extra)
    w = n // freq
    S = jax.ShapeDtypeStruct
    V = pltpu.VMEM
    om, slow = omegas[0], slowness[0]

    sent = (slow - 1.0).astype(BF16)
    got = jnp.stack([shift(sent, "depth", r) for r in range(1, depth)])

    math_scratch = [V((2, h + 8, n), F32), V((2, n, n), F32), V((2, n, n), F32)]
    who = jnp.stack([nf, f0, jnp.where(d == 0, L, 0)]).astype(jnp.int32)
    state, own_a = pl.pallas_call(
        functools.partial(first_levels, (n, slots, L)),
        out_shape=(S((slots, 2, 2, n, n), BF16), S((L, n, n), F32)),
        in_specs=[SM, SM, ANY, ANY, VM, VM, VM, VM],
        out_specs=(ANY, VM),
        scratch_shapes=[V((slots, 2, 2, n, n), F32), V((slots, 2, 2, n, n), BF16)] + math_scratch
        + [pltpu.SemaphoreType.DMA((slots, 2)), pltpu.SemaphoreType.DMA],
        compiler_params=params(32),
        cost_estimate=pl.CostEstimate(flops=8 * 10**9, bytes_accessed=10**7, transcendentals=10**6),
        name="first_levels",
    )(who, om, source[0], receiver[0], slow, T, K2, win)

    who = jnp.stack([nf, f0, jnp.where(d == 0, L, 0), d, fq]).astype(jnp.int32)
    keep_own, send_own, keep_oth, send_oth = pl.pallas_call(
        functools.partial(other_levels, (n, L, depth, freq)),
        out_shape=(S((L, n, w), F32), S((freq - 1, L, n, w), BF16),
                   S((depth - 1, L, n, w), F32), S((freq - 1, depth - 1, L, n, w), BF16)),
        in_specs=[SM, SM, ANY, VM, VM, VM, VM, VM, VM],
        out_specs=(VM, VM, VM, VM),
        scratch_shapes=[V((slots, 2, 2, n, n), BF16), V((n, n), F32), V((n, n), F32)] + math_scratch
        + [pltpu.SemaphoreType.DMA],
        compiler_params=params(32),
        cost_estimate=pl.CostEstimate(flops=8 * 10**9, bytes_accessed=10**7, transcendentals=10**6),
        name="other_levels",
    )(who, om, state, slow, got, own_a, T, K2, win)

    own, oth = keep_own, keep_oth
    for r in range(1, freq):
        oth = oth + shift(send_oth[r - 1], "freq", r).astype(F32)
    for r in range(1, freq):
        own = own + shift(send_own[r - 1], "freq", r).astype(F32)
    oth = oth.astype(BF16)
    arrived = jnp.stack([shift(oth[r - 1], "depth", r) for r in range(1, depth)])

    where = jnp.stack([me, shot_start[0]]).astype(jnp.int32)
    blocks = pl.pallas_call(
        functools.partial(place, (n, L, shots, depth - 1)),
        out_shape=S((shots, L, TILE, w), BF16),
        in_specs=[SM, VM, VM],
        out_specs=VM,
        scratch_shapes=[V((L, 2 * shots * TILE + n, w), F32)],
        compiler_params=params(32),
        name="place",
    )(where, own, arrived)
    pieces = [blocks[0]] + [shift(blocks[r], "shot", r) for r in range(1, shots)]
    return pl.pallas_call(
        functools.partial(gather, (L, shots)),
        out_shape=S((TILE, L, w), F32),
        in_specs=[VM] * shots,
        out_specs=VM,
        compiler_params=params(16),
        name="gather",
    )(*pieces)


def solution(mesh):
    return jax.shard_map(
        local,
        mesh=mesh,
        in_specs=(
            P_(("groups", "shot"), "freq", None, None, None),
            P_(("groups", "shot"), "freq", None, None, None),
            P_(("groups", "shot"), "depth", None, None),
            P_(("groups", "shot"), "freq"),
            P_(("groups", "shot")),
        ),
        out_specs=P_(("groups", "shot"), "depth", "freq"),
        check_vma=False,
    )
```

```python
import functools

import jax
import jax.numpy as jnp
import ml_dtypes
import numpy as np
from jax import lax
from jax.experimental import pallas as pl
from jax.experimental.pallas import tpu as pltpu
from jax.sharding import PartitionSpec as P_

TILE = 128

def _fit(f, hi, deg):
    k = np.arange(400)
    x = (np.cos(np.pi * (k + 0.5) / 400) + 1) / 2 * hi
    c = np.polynomial.chebyshev.Chebyshev.fit(x, f(x), deg, domain=[0, hi])
    return [float(v) for v in c.convert(kind=np.polynomial.Polynomial).coef]
def _cosr(a): return np.cos(np.sqrt(a))
def _sinr(a): return np.sinc(np.sqrt(a) / np.pi)
PC = _fit(_cosr, 12.5, 6); PS = _fit(_sinr, 12.5, 5)
CC = _fit(_cosr, 4.1, 5); CS = _fit(_sinr, 4.1, 4)

def horner(co, x):
    r = co[-1] * x + co[-2]
    for c in co[-3::-1]:
        r = r * x + c
    return r

def make_tables(n):
    h, g = n // 2, n // 4
    idx = np.arange(n)
    ang = 2 * np.pi / n * (np.outer(idx, idx) % n)
    C = np.cos(ang).astype(ml_dtypes.bfloat16).astype(np.float32)
    S = np.sin(ang).astype(ml_dtypes.bfloat16).astype(np.float32)
    i = np.arange(g)
    ev = np.concatenate([2 * i, np.where(i == 0, h, n - 2 * i)])
    od = np.concatenate([2 * i + 1, n - 2 * i - 1])
    out = []
    for k in (ev, od):
        c, s = C[:h][:, k], S[:h][:, k]
        F = np.block([[c, -s], [s, c]])
        L = np.block([[c.T, s.T], [-s.T, c.T]])
        out.append((F, L, F / 1.0, L))
    T = []
    for p in (0, 1):
        k = (ev, od)[p]
        c, s = C[:h][:, k], S[:h][:, k]
        T.append(np.stack([np.block([[c, -s], [s, c]]), np.block([[c.T, s.T], [-s.T, c.T]]),
                           np.block([[c, -s], [s, c]]) / n, np.block([[c.T, s.T], [-s.T, c.T]]) / n]))
    T = np.stack(T, axis=1).astype(ml_dtypes.bfloat16)
    w = ((idx + h) % n - h).astype(np.float32)
    kk = (np.float32(2 * np.pi) / np.float32(n) * w).astype(np.float32)
    k2 = (kk * kk).astype(np.float32)
    base = np.concatenate([k2[2 * i], k2[2 * i + 1]])
    rows = np.concatenate([base, k2[h:h + 1]])
    K2 = np.zeros((h + 8, h), np.float32)
    K2[:h + 1] = rows[:, None] + base[None, :]
    K2[h + 1] = k2[h] + k2[h]
    ed = np.minimum(np.minimum(idx, n - 1 - idx) + 1, n // 16).astype(np.float32) / np.float32(n // 16)
    win = (ed[:, None] * ed[None, :]).astype(np.float32)
    return T, K2, win

def level_prep(n, s, win, D):
    s0 = jnp.sum(s[...]) * (1.0 / (n * n))
    d = s[...] - s0
    D[0] = d * d
    D[1] = d * win[...]
    return s0

def propagator(n, w2, K2, P):
    h, g = n // 2, n // 4
    a = w2 - K2[...]
    pos = a >= 0.0
    r = jnp.sqrt(jnp.abs(a))
    vals = (jnp.where(pos, horner(PC, a), jnp.exp(-r)), jnp.where(pos, r * horner(PS, a), 0.0))
    lane = lax.broadcasted_iota(jnp.int32, (8, h), 1)
    low, mid = lane < g, lane == g
    row0 = lax.broadcasted_iota(jnp.int32, (8, n), 0) == 0
    for comp in (0, 1):
        v = vals[comp]
        col = jnp.broadcast_to(v[h:h + 1], (h, h)).T
        for t in range(h // 8 + 1):
            p = v[8 * t:8 * t + 8]
            q = pltpu.roll(p, g, 1)
            cc = col[8 * t:8 * t + 8] if t < h // 8 else jnp.broadcast_to(v[h + 1:h + 2, :], (8, h))
            e = jnp.where(mid, cc, jnp.where(low, p, q))
            o = jnp.where(low, q, p)
            if t < g // 8:
                P[comp, 8 * t:8 * t + 8, :h] = e
                P[comp, 8 * t:8 * t + 8, h:] = o
                if t == 0:
                    e0, o0 = e, o
            elif t < h // 8:
                P[comp, 8 * t + 8:8 * t + 16, :h] = e
                P[comp, 8 * t + 8:8 * t + 16, h:] = o
            else:
                P[comp, g:g + 8, :h] = jnp.where(row0[:, :h], e, e0)
                P[comp, g:g + 8, h:] = jnp.where(row0[:, :h], o, o0)

def p_rows(n, P, comp, par):
    h, g = n // 2, n // 4
    if par == 0:
        return jnp.concatenate([P[comp, 0:g], P[comp, g:g + 8], P[comp, 8:g]], axis=0)
    o = P[comp, g + 8:h + 8]
    return jnp.concatenate([o, o], axis=0)

def corr(n, om, win, D, c):
    o2 = om * om
    cc, cs, f = [], [], jnp.float32(1.0)
    for k in range(max(len(CC), len(CS))):
        if k < len(CC): cc.append(CC[k] * f)
        if k < len(CS): cs.append(CS[k] * f * om)
        f = f * o2
    x = D[0]
    c[0] = win[...] * horner(cc, x)
    c[1] = D[1] * horner(cs, x)

def front_math(n, om, s0, T, K2, win, st, part, P, c, D):
    h = n // 2
    f32, bf = jnp.float32, jnp.bfloat16
    dot = functools.partial(jnp.dot, preferred_element_type=f32)
    w2 = om * s0; w2 = w2 * w2
    FL = ((0, -1.0), (1, 1.0))
    add, sub = (lambda a, b: a + b), (lambda a, b: a - b)
    def stack2(X, Y, op):
        re = jnp.concatenate([op(X[:h, :h], X[h:, :h]), op(Y[:h, :h], Y[h:, :h])], axis=1)
        im = jnp.concatenate([op(X[:h, h:], X[h:, h:]), op(Y[:h, h:], Y[h:, h:])], axis=1)
        return jnp.concatenate([re, im], axis=0).astype(bf)
    R = []
    for f, sg in FL:
        Ve = dot(st[f, 0], T[0, 0]); Vo = dot(st[f, 1], T[0, 1])
        R.append((stack2(Ve, Vo, add), stack2(Ve, Vo, sub)))
    propagator(n, w2, K2, P)
    W2 = []
    for f, sg in FL:
        out = []
        for p in (0, 1):
            W = dot(T[1, p], R[f][p])
            wr, wi = W[:h], W[h:]
            pr, pi = p_rows(n, P, 0, p), p_rows(n, P, 1, p)
            if sg > 0:
                out.append(jnp.concatenate([wr * pr - wi * pi, wr * pi + wi * pr], axis=0).astype(bf))
            else:
                out.append(jnp.concatenate([wr * pr + wi * pi, wi * pr - wr * pi], axis=0).astype(bf))
        W2.append(out)
    corr(n, om, win, D, c)
    YY = []
    for f, sg in FL:
        E = dot(T[2, 0], W2[f][0]); O = dot(T[2, 1], W2[f][1])
        U, Dn = E + O, E - O
        out = []
        for p in (0, 1):
            sl = slice(p * h, (p + 1) * h)
            out.append(jnp.concatenate([jnp.concatenate([U[:h, sl], U[h:, sl]], axis=1),
                                        jnp.concatenate([Dn[:h, sl], Dn[h:, sl]], axis=1)], axis=0).astype(bf))
        YY.append(out)
    res = []
    for f, sg in FL:
        Q0, Q1 = dot(YY[f][0], T[3, 0]), dot(YY[f][1], T[3, 1])
        X, Z = Q0 + Q1, Q0 - Q1
        halves = []
        for hf, q in ((0, X), (1, Z)):
            qr, qi = q[:, :h], q[:, h:]
            cr, ci = c[0, :, hf * h:(hf + 1) * h], c[1, :, hf * h:(hf + 1) * h]
            if sg > 0:
                halves.append((qr * cr - qi * ci, qr * ci + qi * cr))
            else:
                halves.append((qr * cr + qi * ci, qi * cr - qr * ci))
        (r0, i0), (r1, i1) = halves
        st[f, 0] = jnp.concatenate([r0 + r1, i0 + i1], axis=1).astype(bf)
        st[f, 1] = jnp.concatenate([r0 - r1, i0 - i1], axis=1).astype(bf)
        res.append(halves)
    for hf in (0, 1):
        (ur, ui), (wr, wi) = res[0][hf], res[1][hf]
        sl = slice(hf * h, (hf + 1) * h)
        part[:, sl] = part[:, sl] + (ur * wr + ui * wi)

def prep(n, src, st_ab):
    h = n // 2
    bf = jnp.bfloat16
    st_ab[0] = jnp.concatenate([src[0, :, :h] + src[0, :, h:], src[1, :, :h] + src[1, :, h:]], axis=1).astype(bf)
    st_ab[1] = jnp.concatenate([src[0, :, :h] - src[0, :, h:], src[1, :, :h] - src[1, :, h:]], axis=1).astype(bf)


HBM = pl.BlockSpec(memory_space=pltpu.HBM)
VM = pl.BlockSpec(memory_space=pltpu.VMEM)
SM = pl.BlockSpec(memory_space=pltpu.SMEM)
F32, BF16 = jnp.float32, jnp.bfloat16


def params(mib):
    return pltpu.CompilerParams(vmem_limit_bytes=mib * 1024 * 1024)


def share(fronts, depth):
    d = lax.axis_index("depth")
    base, extra = fronts // depth, fronts % depth
    return d, base + jnp.where(d < extra, 1, 0), d * base + jnp.minimum(d, extra)


def first_levels(dims, om_h, src, rcv, slow_h, T_h, K2_h, win_h, st, own_out,
                 om, raw, slow, T, K2, win, P, c, D, sem_in, sem_t):
    n, slots, L, fronts, depth = dims
    d, nf, f0 = share(fronts, depth)

    def moves(j):
        fr = jnp.minimum(f0 + j, fronts - 1)
        return (
            pltpu.make_async_copy(src.at[fr], raw.at[j, 0], sem_in.at[j, 0]),
            pltpu.make_async_copy(rcv.at[fr], raw.at[j, 1], sem_in.at[j, 1]),
        )

    tables = [
        pltpu.make_async_copy(a, b, sem_t.at[i])
        for i, (a, b) in enumerate(((om_h, om), (slow_h, slow), (T_h, T), (K2_h, K2), (win_h, win)))
    ]
    for j in range(slots):
        for m in moves(j):
            m.start()
        if j == 0:
            for m in tables:
                m.start()
    for j in range(slots):
        for f, m in enumerate(moves(j)):
            m.wait()
            prep(n, raw.at[j, f], st.at[j, f])
    for m in tables:
        m.wait()

    def level(z, _):
        s0 = level_prep(n, slow.at[z], win, D)
        own_out[z] = jnp.zeros((n, n), F32)

        def front(j, _):
            front_math(n, om[0, f0 + j], s0, T, K2, win, st.at[j], own_out.at[z], P, c, D)
            return 0

        lax.fori_loop(0, nf, front, 0)
        return 0

    lax.fori_loop(0, jnp.where(d == 0, L, 0), level, 0)


def other_levels(dims, om, st_in, slow, got, own_in, T, K2, win, keep_own, send_own, keep_oth, send_oth, st,
                 s_now, part, P, c, D):
    n, L, fronts, depth, freq = dims
    d, nf, f0 = share(fronts, depth)
    fq = lax.axis_index("freq")
    lo = jnp.where(d == 0, L, 0)
    w = n // freq

    def split(ref, keep, sends):
        for a in range(freq):
            @pl.when(fq == a)
            def _():
                keep[...] = ref[:, a * w:(a + 1) * w]
                for r in range(1, freq):
                    b = (a + r) % freq
                    sends.at[r - 1][...] = ref[:, b * w:(b + 1) * w].astype(BF16)

    @pl.when(lo > 0)
    def _():
        for z in range(L):
            split(own_in.at[z], keep_own.at[z], send_own.at[:, z])

    def level(z, _):
        owner = z // L
        zl = z - owner * L
        back = lax.rem(d - owner + depth, depth)

        @pl.when(back == 0)
        def _():
            s_now[...] = slow[zl]

        @pl.when(back > 0)
        def _():
            s_now[...] = got[jnp.maximum(back - 1, 0), zl].astype(F32) + 1.0

        s0 = level_prep(n, s_now, win, D)
        part[...] = jnp.zeros((n, n), F32)

        def front(j, _):
            front_math(n, om[0, f0 + j], s0, T, K2, win, st.at[j], part, P, c, D)
            return 0

        lax.fori_loop(0, nf, front, 0)

        @pl.when(back == 0)
        def _():
            split(part, keep_own.at[zl], send_own.at[:, zl])

        @pl.when(back > 0)
        def _():
            r = jnp.maximum(depth - back - 1, 0)
            split(part, keep_oth.at[r, zl], send_oth.at[:, r, zl])

        return 0

    lax.fori_loop(lo, depth * L, level, 0)


def place(dims, start, own, got, out, padded):
    n, L, shots, more = dims
    w = own.shape[-1]
    survey = shots * TILE
    me, begin = lax.axis_index("shot"), start[0]
    padded[:, :survey] = jnp.zeros((L, survey, w), F32)
    padded[:, survey + n:] = jnp.zeros((L, survey, w), F32)
    for z in range(L):
        total = own[z]
        for r in range(more):
            total = total + got[r, z].astype(F32)
        padded[z, survey:survey + n] = total
    for r in range(shots):
        owner = lax.rem(me + r, shots)
        offset = jnp.clip(owner * TILE - begin + survey, 0, n + survey)
        for z in range(L):
            out[r, z] = padded[z, pl.ds(offset, TILE), :].astype(BF16)


def gather(dims, *refs):
    L, shots = dims
    out = refs[-1]
    for z in range(L):
        total = refs[0][z].astype(F32)
        for r in range(1, shots):
            total = total + refs[r][z].astype(F32)
        out[:, z, :] = total


def shift(array, axis, by):
    size = lax.axis_size(axis)
    return lax.ppermute(array, axis, [(i, (i + by) % size) for i in range(size)])


def local(source, receiver, slowness, omegas, shot_start):
    n = source.shape[-1]
    h = n // 2
    fronts, L = source.shape[1], slowness.shape[1]
    depth, freq, shots = lax.axis_size("depth"), lax.axis_size("freq"), lax.axis_size("shot")
    T, K2, win = make_tables(n)
    slots = -(-fronts // depth)
    w = n // freq
    S = jax.ShapeDtypeStruct
    V = pltpu.VMEM
    slow = slowness[0]

    sent = (slow - 1.0).astype(BF16)
    got = jnp.stack([shift(sent, "depth", r) for r in range(1, depth)])

    math_scratch = [V((2, h + 8, n), F32), V((2, n, n), F32), V((2, n, n), F32)]
    state, own_a = pl.pallas_call(
        functools.partial(first_levels, (n, slots, L, fronts, depth)),
        out_shape=(S((slots, 2, 2, n, n), BF16), S((L, n, n), F32)),
        in_specs=[HBM] * 7,
        out_specs=(VM, VM),
        scratch_shapes=[pltpu.SMEM((1, fronts), F32), V((slots, 2, 2, n, n), F32), V((L, n, n), F32),
                        V((4, 2, n, n), BF16), V((h + 8, h), F32), V((n, n), F32)] + math_scratch
        + [pltpu.SemaphoreType.DMA((slots, 2)), pltpu.SemaphoreType.DMA((5,))],
        compiler_params=params(50),
        cost_estimate=pl.CostEstimate(flops=8 * 10**9, bytes_accessed=10**7, transcendentals=10**6),
        name="first_levels",
    )(omegas, source[0], receiver[0], slow, T, K2, win)

    keep_own, send_own, keep_oth, send_oth, _ = pl.pallas_call(
        functools.partial(other_levels, (n, L, fronts, depth, freq)),
        out_shape=(S((L, n, w), F32), S((freq - 1, L, n, w), BF16),
                   S((depth - 1, L, n, w), F32), S((freq - 1, depth - 1, L, n, w), BF16),
                   S(state.shape, state.dtype)),
        in_specs=[SM, VM, VM, VM, VM, VM, VM, VM],
        out_specs=(VM, VM, VM, VM, VM),
        input_output_aliases={1: 4},
        scratch_shapes=[V((n, n), F32), V((n, n), F32)] + math_scratch,
        compiler_params=params(32),
        cost_estimate=pl.CostEstimate(flops=8 * 10**9, bytes_accessed=10**7, transcendentals=10**6),
        name="other_levels",
    )(omegas, state, slow, got, own_a, T, K2, win)

    own, oth = keep_own, keep_oth
    for r in range(1, freq):
        oth = oth + shift(send_oth[r - 1], "freq", r).astype(F32)
    for r in range(1, freq):
        own = own + shift(send_own[r - 1], "freq", r).astype(F32)
    oth = oth.astype(BF16)
    arrived = jnp.stack([shift(oth[r - 1], "depth", r) for r in range(1, depth)])

    blocks = pl.pallas_call(
        functools.partial(place, (n, L, shots, depth - 1)),
        out_shape=S((shots, L, TILE, w), BF16),
        in_specs=[SM, VM, VM],
        out_specs=VM,
        scratch_shapes=[V((L, 2 * shots * TILE + n, w), F32)],
        compiler_params=params(32),
        name="place",
    )(shot_start, own, arrived)
    pieces = [blocks[0]] + [shift(blocks[r], "shot", r) for r in range(1, shots)]
    return pl.pallas_call(
        functools.partial(gather, (L, shots)),
        out_shape=S((TILE, L, w), F32),
        in_specs=[VM] * shots,
        out_specs=VM,
        compiler_params=params(16),
        name="gather",
    )(*pieces)


def solution(mesh):
    return jax.shard_map(
        local,
        mesh=mesh,
        in_specs=(
            P_(("groups", "shot"), "freq", None, None, None),
            P_(("groups", "shot"), "freq", None, None, None),
            P_(("groups", "shot"), "depth", None, None),
            P_(("groups", "shot"), "freq"),
            P_(("groups", "shot")),
        ),
        out_specs=P_(("groups", "shot"), "depth", "freq"),
        check_vma=False,
    )
```

```python
import functools

import jax
import jax.numpy as jnp
import ml_dtypes
import numpy as np
from jax import lax
from jax.experimental import pallas as pl
from jax.experimental.pallas import tpu as pltpu
from jax.sharding import PartitionSpec as P_

TILE = 128

def _fit(f, hi, deg):
    k = np.arange(400)
    x = (np.cos(np.pi * (k + 0.5) / 400) + 1) / 2 * hi
    c = np.polynomial.chebyshev.Chebyshev.fit(x, f(x), deg, domain=[0, hi])
    return [float(v) for v in c.convert(kind=np.polynomial.Polynomial).coef]
def _cosr(a): return np.cos(np.sqrt(a))
def _sinr(a): return np.sinc(np.sqrt(a) / np.pi)
PC = _fit(_cosr, 12.5, 6); PS = _fit(_sinr, 12.5, 5)
CC = _fit(_cosr, 4.1, 5); CS = _fit(_sinr, 4.1, 4)

def horner(co, x):
    r = co[-1] * x + co[-2]
    for c in co[-3::-1]:
        r = r * x + c
    return r

def make_tables(n):
    h, g = n // 2, n // 4
    idx = np.arange(n)
    ang = 2 * np.pi / n * (np.outer(idx, idx) % n)
    C = np.cos(ang).astype(ml_dtypes.bfloat16).astype(np.float32)
    S = np.sin(ang).astype(ml_dtypes.bfloat16).astype(np.float32)
    i = np.arange(g)
    ev = np.concatenate([2 * i, np.where(i == 0, h, n - 2 * i)])
    od = np.concatenate([2 * i + 1, n - 2 * i - 1])
    out = []
    for k in (ev, od):
        c, s = C[:h][:, k], S[:h][:, k]
        F = np.block([[c, -s], [s, c]])
        L = np.block([[c.T, s.T], [-s.T, c.T]])
        out.append((F, L, F / 1.0, L))
    T = []
    for p in (0, 1):
        k = (ev, od)[p]
        c, s = C[:h][:, k], S[:h][:, k]
        T.append(np.stack([np.block([[c, -s], [s, c]]), np.block([[c.T, s.T], [-s.T, c.T]]),
                           np.block([[c, -s], [s, c]]) / n, np.block([[c.T, s.T], [-s.T, c.T]]) / n]))
    T = np.stack(T, axis=1).astype(ml_dtypes.bfloat16)
    w = ((idx + h) % n - h).astype(np.float32)
    kk = (np.float32(2 * np.pi) / np.float32(n) * w).astype(np.float32)
    k2 = (kk * kk).astype(np.float32)
    base = np.concatenate([k2[2 * i], k2[2 * i + 1]])
    rows = np.concatenate([base, k2[h:h + 1]])
    K2 = np.zeros((h + 8, h), np.float32)
    K2[:h + 1] = rows[:, None] + base[None, :]
    K2[h + 1] = k2[h] + k2[h]
    ed = np.minimum(np.minimum(idx, n - 1 - idx) + 1, n // 16).astype(np.float32) / np.float32(n // 16)
    win = (ed[:, None] * ed[None, :]).astype(np.float32)
    return T, K2, win

def level_prep(n, s, win, D):
    s0 = jnp.sum(s[...]) * (1.0 / (n * n))
    d = s[...] - s0
    D[0] = d * d
    D[1] = d * win[...]
    return s0

def propagator(n, w2, K2, P):
    h, g = n // 2, n // 4
    a = w2 - K2[...]
    pos = a >= 0.0
    r = jnp.sqrt(jnp.abs(a))
    vals = (jnp.where(pos, horner(PC, a), jnp.exp(-r)), jnp.where(pos, r * horner(PS, a), 0.0))
    lane = lax.broadcasted_iota(jnp.int32, (8, h), 1)
    low, mid = lane < g, lane == g
    row0 = lax.broadcasted_iota(jnp.int32, (8, n), 0) == 0
    for comp in (0, 1):
        v = vals[comp]
        col = jnp.broadcast_to(v[h:h + 1], (h, h)).T
        for t in range(h // 8 + 1):
            p = v[8 * t:8 * t + 8]
            q = pltpu.roll(p, g, 1)
            cc = col[8 * t:8 * t + 8] if t < h // 8 else jnp.broadcast_to(v[h + 1:h + 2, :], (8, h))
            e = jnp.where(mid, cc, jnp.where(low, p, q))
            o = jnp.where(low, q, p)
            if t < g // 8:
                P[comp, 8 * t:8 * t + 8, :h] = e
                P[comp, 8 * t:8 * t + 8, h:] = o
                if t == 0:
                    e0, o0 = e, o
            elif t < h // 8:
                P[comp, 8 * t + 8:8 * t + 16, :h] = e
                P[comp, 8 * t + 8:8 * t + 16, h:] = o
            else:
                P[comp, g:g + 8, :h] = jnp.where(row0[:, :h], e, e0)
                P[comp, g:g + 8, h:] = jnp.where(row0[:, :h], o, o0)

def p_rows(n, P, comp, par):
    h, g = n // 2, n // 4
    if par == 0:
        return jnp.concatenate([P[comp, 0:g], P[comp, g:g + 8], P[comp, 8:g]], axis=0)
    o = P[comp, g + 8:h + 8]
    return jnp.concatenate([o, o], axis=0)

def corr(n, om, win, D, c):
    o2 = om * om
    cc, cs, f = [], [], jnp.float32(1.0)
    for k in range(max(len(CC), len(CS))):
        if k < len(CC): cc.append(CC[k] * f)
        if k < len(CS): cs.append(CS[k] * f * om)
        f = f * o2
    x = D[0]
    c[0] = win[...] * horner(cc, x)
    c[1] = D[1] * horner(cs, x)

def front_math(n, om, s0, T, K2, win, st, part, P, c, D):
    h = n // 2
    f32, bf = jnp.float32, jnp.bfloat16
    dot = functools.partial(jnp.dot, preferred_element_type=f32)
    w2 = om * s0; w2 = w2 * w2
    FL = ((0, -1.0), (1, 1.0))
    add, sub = (lambda a, b: a + b), (lambda a, b: a - b)
    def stack2(X, Y, op):
        re = jnp.concatenate([op(X[:h, :h], X[h:, :h]), op(Y[:h, :h], Y[h:, :h])], axis=1)
        im = jnp.concatenate([op(X[:h, h:], X[h:, h:]), op(Y[:h, h:], Y[h:, h:])], axis=1)
        return jnp.concatenate([re, im], axis=0).astype(bf)
    R = []
    for f, sg in FL:
        Ve = dot(st[f, 0], T[0, 0]); Vo = dot(st[f, 1], T[0, 1])
        R.append((stack2(Ve, Vo, add), stack2(Ve, Vo, sub)))
    propagator(n, w2, K2, P)
    W2 = []
    for f, sg in FL:
        out = []
        for p in (0, 1):
            W = dot(T[1, p], R[f][p])
            wr, wi = W[:h], W[h:]
            pr, pi = p_rows(n, P, 0, p), p_rows(n, P, 1, p)
            if sg > 0:
                out.append(jnp.concatenate([wr * pr - wi * pi, wr * pi + wi * pr], axis=0).astype(bf))
            else:
                out.append(jnp.concatenate([wr * pr + wi * pi, wi * pr - wr * pi], axis=0).astype(bf))
        W2.append(out)
    corr(n, om, win, D, c)
    YY = []
    for f, sg in FL:
        E = dot(T[2, 0], W2[f][0]); O = dot(T[2, 1], W2[f][1])
        U, Dn = E + O, E - O
        out = []
        for p in (0, 1):
            sl = slice(p * h, (p + 1) * h)
            out.append(jnp.concatenate([jnp.concatenate([U[:h, sl], U[h:, sl]], axis=1),
                                        jnp.concatenate([Dn[:h, sl], Dn[h:, sl]], axis=1)], axis=0).astype(bf))
        YY.append(out)
    res = []
    for f, sg in FL:
        Q0, Q1 = dot(YY[f][0], T[3, 0]), dot(YY[f][1], T[3, 1])
        X, Z = Q0 + Q1, Q0 - Q1
        halves = []
        for hf, q in ((0, X), (1, Z)):
            qr, qi = q[:, :h], q[:, h:]
            cr, ci = c[0, :, hf * h:(hf + 1) * h], c[1, :, hf * h:(hf + 1) * h]
            if sg > 0:
                halves.append((qr * cr - qi * ci, qr * ci + qi * cr))
            else:
                halves.append((qr * cr + qi * ci, qi * cr - qr * ci))
        (r0, i0), (r1, i1) = halves
        st[f, 0] = jnp.concatenate([r0 + r1, i0 + i1], axis=1).astype(bf)
        st[f, 1] = jnp.concatenate([r0 - r1, i0 - i1], axis=1).astype(bf)
        res.append(halves)
    for hf in (0, 1):
        (ur, ui), (wr, wi) = res[0][hf], res[1][hf]
        sl = slice(hf * h, (hf + 1) * h)
        part[:, sl] = part[:, sl] + (ur * wr + ui * wi)

def prep(n, src, st_ab):
    h = n // 2
    bf = jnp.bfloat16
    st_ab[0] = jnp.concatenate([src[0, :, :h] + src[0, :, h:], src[1, :, :h] + src[1, :, h:]], axis=1).astype(bf)
    st_ab[1] = jnp.concatenate([src[0, :, :h] - src[0, :, h:], src[1, :, :h] - src[1, :, h:]], axis=1).astype(bf)


HBM = pl.BlockSpec(memory_space=pltpu.HBM)
VM = pl.BlockSpec(memory_space=pltpu.VMEM)
SM = pl.BlockSpec(memory_space=pltpu.SMEM)
F32, BF16 = jnp.float32, jnp.bfloat16


def params(mib):
    return pltpu.CompilerParams(vmem_limit_bytes=mib * 1024 * 1024)


def share(fronts, depth):
    d = lax.axis_index("depth")
    base, extra = fronts // depth, fronts % depth
    return d, base + jnp.where(d < extra, 1, 0), d * base + jnp.minimum(d, extra)


def first_levels(dims, om_h, src, rcv, slow_h, T_h, K2_h, win_h, st, own_out, slow, T, K2, win, om_out,
                 om, raw, P, c, D, sem_in, sem_t):
    n, slots, L, fronts, depth = dims
    d, nf, f0 = share(fronts, depth)

    def moves(j):
        fr = jnp.minimum(f0 + j, fronts - 1)
        return (
            pltpu.make_async_copy(src.at[fr], raw.at[j, 0], sem_in.at[j, 0]),
            pltpu.make_async_copy(rcv.at[fr], raw.at[j, 1], sem_in.at[j, 1]),
        )

    tables = [
        pltpu.make_async_copy(a, b, sem_t.at[i])
        for i, (a, b) in enumerate(((om_h, om), (slow_h, slow), (T_h, T), (K2_h, K2), (win_h, win)))
    ]
    for j in range(slots):
        for m in moves(j):
            m.start()
        if j == 0:
            for m in tables:
                m.start()
    for j in range(slots):
        for f, m in enumerate(moves(j)):
            m.wait()
            prep(n, raw.at[j, f], st.at[j, f])
    for m in tables:
        m.wait()
    for f in range(fronts):
        om_out[0, f] = om[0, f]

    def level(z, _):
        s0 = level_prep(n, slow.at[z], win, D)
        own_out[z] = jnp.zeros((n, n), F32)

        def front(j, _):
            front_math(n, om[0, f0 + j], s0, T, K2, win, st.at[j], own_out.at[z], P, c, D)
            return 0

        lax.fori_loop(0, nf, front, 0)
        return 0

    lax.fori_loop(0, jnp.where(d == 0, L, 0), level, 0)


def other_levels(dims, om, st_in, slow, got, own_in, T, K2, win, keep_own, send_own, keep_oth, send_oth, st,
                 s_now, part, P, c, D):
    n, L, fronts, depth, freq = dims
    d, nf, f0 = share(fronts, depth)
    fq = lax.axis_index("freq")
    lo = jnp.where(d == 0, L, 0)
    w = n // freq

    def split(ref, keep, sends):
        for a in range(freq):
            @pl.when(fq == a)
            def _():
                keep[...] = ref[:, a * w:(a + 1) * w]
                for r in range(1, freq):
                    b = (a + r) % freq
                    sends.at[r - 1][...] = ref[:, b * w:(b + 1) * w].astype(BF16)

    @pl.when(lo > 0)
    def _():
        for z in range(L):
            split(own_in.at[z], keep_own.at[z], send_own.at[:, z])

    def level(z, _):
        owner = z // L
        zl = z - owner * L
        back = lax.rem(d - owner + depth, depth)

        @pl.when(back == 0)
        def _():
            s_now[...] = slow[zl]

        @pl.when(back > 0)
        def _():
            s_now[...] = got[jnp.maximum(back - 1, 0), zl].astype(F32) + 1.0

        s0 = level_prep(n, s_now, win, D)
        part[...] = jnp.zeros((n, n), F32)

        def front(j, _):
            front_math(n, om[0, f0 + j], s0, T, K2, win, st.at[j], part, P, c, D)
            return 0

        lax.fori_loop(0, nf, front, 0)

        @pl.when(back == 0)
        def _():
            split(part, keep_own.at[zl], send_own.at[:, zl])

        @pl.when(back > 0)
        def _():
            r = jnp.maximum(depth - back - 1, 0)
            split(part, keep_oth.at[r, zl], send_oth.at[:, r, zl])

        return 0

    lax.fori_loop(lo, depth * L, level, 0)


def place(dims, start, own, got, out, padded):
    n, L, shots, more = dims
    w = own.shape[-1]
    survey = shots * TILE
    me, begin = lax.axis_index("shot"), start[0]
    padded[:, :survey] = jnp.zeros((L, survey, w), F32)
    padded[:, survey + n:] = jnp.zeros((L, survey, w), F32)
    for z in range(L):
        total = own[z]
        for r in range(more):
            total = total + got[r, z].astype(F32)
        padded[z, survey:survey + n] = total
    for r in range(shots):
        owner = lax.rem(me + r, shots)
        offset = jnp.clip(owner * TILE - begin + survey, 0, n + survey)
        for z in range(L):
            out[r, z] = padded[z, pl.ds(offset, TILE), :].astype(BF16)


def gather(dims, *refs):
    L, shots = dims
    out = refs[-1]
    for z in range(L):
        total = refs[0][z].astype(F32)
        for r in range(1, shots):
            total = total + refs[r][z].astype(F32)
        out[:, z, :] = total


def shift(array, axis, by):
    size = lax.axis_size(axis)
    return lax.ppermute(array, axis, [(i, (i + by) % size) for i in range(size)])


def local(source, receiver, slowness, omegas, shot_start):
    n = source.shape[-1]
    h = n // 2
    fronts, L = source.shape[1], slowness.shape[1]
    depth, freq, shots = lax.axis_size("depth"), lax.axis_size("freq"), lax.axis_size("shot")
    T, K2, win = make_tables(n)
    slots = -(-fronts // depth)
    w = n // freq
    S = jax.ShapeDtypeStruct
    V = pltpu.VMEM
    slow = slowness[0]

    sent = (slow - 1.0).astype(BF16)
    got = jnp.stack([shift(sent, "depth", r) for r in range(1, depth)])

    math_scratch = [V((2, h + 8, n), F32), V((2, n, n), F32), V((2, n, n), F32)]
    state, own_a, slow_v, T_v, K2_v, win_v, om = pl.pallas_call(
        functools.partial(first_levels, (n, slots, L, fronts, depth)),
        out_shape=(S((slots, 2, 2, n, n), BF16), S((L, n, n), F32), S((L, n, n), F32), S((4, 2, n, n), BF16),
                   S((h + 8, h), F32), S((n, n), F32), S((1, fronts), F32)),
        in_specs=[HBM] * 7,
        out_specs=(VM, VM, VM, VM, VM, VM, SM),
        scratch_shapes=[pltpu.SMEM((1, fronts), F32), V((slots, 2, 2, n, n), F32)] + math_scratch
        + [pltpu.SemaphoreType.DMA((slots, 2)), pltpu.SemaphoreType.DMA((5,))],
        compiler_params=params(40),
        cost_estimate=pl.CostEstimate(flops=8 * 10**9, bytes_accessed=10**7, transcendentals=10**6),
        name="first_levels",
    )(*[pltpu.with_memory_space_constraint(a, pltpu.HBM) for a in (omegas, source[0], receiver[0], slow, jnp.asarray(T), jnp.asarray(K2), jnp.asarray(win))])

    keep_own, send_own, keep_oth, send_oth, _ = pl.pallas_call(
        functools.partial(other_levels, (n, L, fronts, depth, freq)),
        out_shape=(S((L, n, w), F32), S((freq - 1, L, n, w), BF16),
                   S((depth - 1, L, n, w), F32), S((freq - 1, depth - 1, L, n, w), BF16),
                   S(state.shape, state.dtype)),
        in_specs=[SM, VM, VM, VM, VM, VM, VM, VM],
        out_specs=(VM, VM, VM, VM, VM),
        input_output_aliases={1: 4},
        scratch_shapes=[V((n, n), F32), V((n, n), F32)] + math_scratch,
        compiler_params=params(32),
        cost_estimate=pl.CostEstimate(flops=8 * 10**9, bytes_accessed=10**7, transcendentals=10**6),
        name="other_levels",
    )(om, state, slow_v, got, own_a, T_v, K2_v, win_v)

    own, oth = keep_own, keep_oth
    for r in range(1, freq):
        oth = oth + shift(send_oth[r - 1], "freq", r).astype(F32)
    for r in range(1, freq):
        own = own + shift(send_own[r - 1], "freq", r).astype(F32)
    oth = oth.astype(BF16)
    arrived = jnp.stack([shift(oth[r - 1], "depth", r) for r in range(1, depth)])

    blocks = pl.pallas_call(
        functools.partial(place, (n, L, shots, depth - 1)),
        out_shape=S((shots, L, TILE, w), BF16),
        in_specs=[SM, VM, VM],
        out_specs=VM,
        scratch_shapes=[V((L, 2 * shots * TILE + n, w), F32)],
        compiler_params=params(32),
        name="place",
    )(shot_start, own, arrived)
    pieces = [blocks[0]] + [shift(blocks[r], "shot", r) for r in range(1, shots)]
    return pl.pallas_call(
        functools.partial(gather, (L, shots)),
        out_shape=S((TILE, L, w), F32),
        in_specs=[VM] * shots,
        out_specs=VM,
        compiler_params=params(16),
        name="gather",
    )(*pieces)


def solution(mesh):
    return jax.shard_map(
        local,
        mesh=mesh,
        in_specs=(
            P_(("groups", "shot"), "freq", None, None, None),
            P_(("groups", "shot"), "freq", None, None, None),
            P_(("groups", "shot"), "depth", None, None),
            P_(("groups", "shot"), "freq"),
            P_(("groups", "shot")),
        ),
        out_specs=P_(("groups", "shot"), "depth", "freq"),
        check_vma=False,
    )
```

```python
import functools

import jax
import jax.numpy as jnp
import ml_dtypes
import numpy as np
from jax import lax
from jax.experimental import pallas as pl
from jax.experimental.pallas import tpu as pltpu
from jax.sharding import PartitionSpec as P_

TILE = 128

def _fit(f, hi, deg):
    k = np.arange(400)
    x = (np.cos(np.pi * (k + 0.5) / 400) + 1) / 2 * hi
    c = np.polynomial.chebyshev.Chebyshev.fit(x, f(x), deg, domain=[0, hi])
    return [float(v) for v in c.convert(kind=np.polynomial.Polynomial).coef]
def _cosr(a): return np.cos(np.sqrt(a))
def _sinr(a): return np.sinc(np.sqrt(a) / np.pi)
PC = _fit(_cosr, 12.5, 6); PS = _fit(_sinr, 12.5, 5)
CC = _fit(lambda a: (_cosr(a) - 1) / a, 4.1, 4); CS = _fit(_sinr, 4.1, 4)

def horner(co, x):
    r = co[-1] * x + co[-2]
    for c in co[-3::-1]:
        r = r * x + c
    return r

def make_tables(n):
    h, g = n // 2, n // 4
    idx = np.arange(n)
    ang = 2 * np.pi / n * (np.outer(idx, idx) % n)
    C = np.cos(ang).astype(ml_dtypes.bfloat16).astype(np.float32)
    S = np.sin(ang).astype(ml_dtypes.bfloat16).astype(np.float32)
    i = np.arange(g)
    ev = np.concatenate([2 * i, np.where(i == 0, h, n - 2 * i)])
    od = np.concatenate([2 * i + 1, n - 2 * i - 1])
    out = []
    for k in (ev, od):
        c, s = C[:h][:, k], S[:h][:, k]
        F = np.block([[c, -s], [s, c]])
        L = np.block([[c.T, s.T], [-s.T, c.T]])
        out.append((F, L, F / 1.0, L))
    T = []
    for p in (0, 1):
        k = (ev, od)[p]
        c, s = C[:h][:, k], S[:h][:, k]
        T.append(np.stack([np.block([[c, -s], [s, c]]), np.block([[c.T, s.T], [-s.T, c.T]]),
                           np.block([[c, -s], [s, c]]) / n, np.block([[c.T, s.T], [-s.T, c.T]]) / n]))
    T = np.stack(T, axis=1).astype(ml_dtypes.bfloat16)
    w = ((idx + h) % n - h).astype(np.float32)
    kk = (np.float32(2 * np.pi) / np.float32(n) * w).astype(np.float32)
    k2 = (kk * kk).astype(np.float32)
    base = np.concatenate([k2[2 * i], k2[2 * i + 1]])
    rows = np.concatenate([base, k2[h:h + 1]])
    K2 = np.zeros((h + 8, h), np.float32)
    K2[:h + 1] = rows[:, None] + base[None, :]
    K2[h + 1] = k2[h] + k2[h]
    ed = np.minimum(np.minimum(idx, n - 1 - idx) + 1, n // 16).astype(np.float32) / np.float32(n // 16)
    win = (ed[:, None] * ed[None, :]).astype(np.float32)
    return T, K2, win

def level_prep(n, s, win, D):
    s0 = jnp.sum(s[...]) * (1.0 / (n * n))
    d = s[...] - s0
    x = d * d
    D[0] = x
    D[1] = d * win[...]
    D[2] = x * win[...]
    return s0

def propagator(n, w2, K2, P):
    h, g = n // 2, n // 4
    a = w2 - K2[...]
    pos = a >= 0.0
    r = jnp.sqrt(jnp.abs(a))
    vals = (jnp.where(pos, horner(PC, a), jnp.exp(-r)), jnp.where(pos, r * horner(PS, a), 0.0))
    lane = lax.broadcasted_iota(jnp.int32, (8, h), 1)
    low, mid = lane < g, lane == g
    row0 = lax.broadcasted_iota(jnp.int32, (8, n), 0) == 0
    for comp in (0, 1):
        v = vals[comp]
        col = jnp.broadcast_to(v[h:h + 1], (h, h)).T
        for t in range(h // 8 + 1):
            p = v[8 * t:8 * t + 8]
            q = pltpu.roll(p, g, 1)
            cc = col[8 * t:8 * t + 8] if t < h // 8 else jnp.broadcast_to(v[h + 1:h + 2, :], (8, h))
            e = jnp.where(mid, cc, jnp.where(low, p, q))
            o = jnp.where(low, q, p)
            if t < g // 8:
                P[comp, 8 * t:8 * t + 8, :h] = e
                P[comp, 8 * t:8 * t + 8, h:] = o
                if t == 0:
                    e0, o0 = e, o
            elif t < h // 8:
                P[comp, 8 * t + 8:8 * t + 16, :h] = e
                P[comp, 8 * t + 8:8 * t + 16, h:] = o
            else:
                P[comp, g:g + 8, :h] = jnp.where(row0[:, :h], e, e0)
                P[comp, g:g + 8, h:] = jnp.where(row0[:, :h], o, o0)

def p_rows(n, P, comp, par):
    h, g = n // 2, n // 4
    if par == 0:
        return jnp.concatenate([P[comp, 0:g], P[comp, g:g + 8], P[comp, 8:g]], axis=0)
    o = P[comp, g + 8:h + 8]
    return jnp.concatenate([o, o], axis=0)

def corr(om, win, D, c):
    cc, cs, f = [], [], om
    for k in range(len(CC)):
        cs.append(CS[k] * f)
        f = f * om
        cc.append(CC[k] * f)
        f = f * om
    x = D[0]
    c[0] = win[...] + D[2] * horner(cc, x)
    c[1] = D[1] * horner(cs, x)

def front_math(n, om, s0, T, K2, win, st, P, c, D):
    h = n // 2
    f32, bf = jnp.float32, jnp.bfloat16
    dot = functools.partial(jnp.dot, preferred_element_type=f32)
    w2 = om * s0; w2 = w2 * w2
    FL = ((0, -1.0), (1, 1.0))
    add, sub = (lambda a, b: a + b), (lambda a, b: a - b)
    def stack2(X, Y, op):
        re = jnp.concatenate([op(X[:h, :h], X[h:, :h]), op(Y[:h, :h], Y[h:, :h])], axis=1)
        im = jnp.concatenate([op(X[:h, h:], X[h:, h:]), op(Y[:h, h:], Y[h:, h:])], axis=1)
        return jnp.concatenate([re, im], axis=0).astype(bf)
    R = []
    for f, sg in FL:
        Ve = dot(st[f, 0], T[0, 0]); Vo = dot(st[f, 1], T[0, 1])
        R.append((stack2(Ve, Vo, add), stack2(Ve, Vo, sub)))
    propagator(n, w2, K2, P)
    W2 = []
    for f, sg in FL:
        out = []
        for p in (0, 1):
            W = dot(T[1, p], R[f][p])
            wr, wi = W[:h], W[h:]
            pr, pi = p_rows(n, P, 0, p), p_rows(n, P, 1, p)
            if sg > 0:
                out.append(jnp.concatenate([wr * pr - wi * pi, wr * pi + wi * pr], axis=0).astype(bf))
            else:
                out.append(jnp.concatenate([wr * pr + wi * pi, wi * pr - wr * pi], axis=0).astype(bf))
        W2.append(out)
    corr(om, win, D, c)
    YY = []
    for f, sg in FL:
        E = dot(T[2, 0], W2[f][0]); O = dot(T[2, 1], W2[f][1])
        U, Dn = E + O, E - O
        out = []
        for p in (0, 1):
            sl = slice(p * h, (p + 1) * h)
            out.append(jnp.concatenate([jnp.concatenate([U[:h, sl], U[h:, sl]], axis=1),
                                        jnp.concatenate([Dn[:h, sl], Dn[h:, sl]], axis=1)], axis=0).astype(bf))
        YY.append(out)
    res = []
    for f, sg in FL:
        Q0, Q1 = dot(YY[f][0], T[3, 0]), dot(YY[f][1], T[3, 1])
        X, Z = Q0 + Q1, Q0 - Q1
        halves = []
        for hf, q in ((0, X), (1, Z)):
            qr, qi = q[:, :h], q[:, h:]
            cr, ci = c[0, :, hf * h:(hf + 1) * h], c[1, :, hf * h:(hf + 1) * h]
            if sg > 0:
                halves.append((qr * cr - qi * ci, qr * ci + qi * cr))
            else:
                halves.append((qr * cr + qi * ci, qi * cr - qr * ci))
        (r0, i0), (r1, i1) = halves
        st[f, 0] = jnp.concatenate([r0 + r1, i0 + i1], axis=1).astype(bf)
        st[f, 1] = jnp.concatenate([r0 - r1, i0 - i1], axis=1).astype(bf)
        res.append(halves)
    terms = []
    for hf in (0, 1):
        (ur, ui), (wr, wi) = res[0][hf], res[1][hf]
        terms.append(ur * wr + ui * wi)
    return terms


def level_math(n, oms, s, T, K2, win, st, part, P, c, D):
    h = n // 2
    s0 = level_prep(n, s, win, D)
    terms = [front_math(n, om, s0, T, K2, win, st.at[j], P.at[j], c.at[j], D) for j, om in enumerate(oms)]
    for hf in (0, 1):
        part[:, hf * h:(hf + 1) * h] = functools.reduce(lambda a, b: a + b, [t[hf] for t in terms])


def prep(n, src, st_ab):
    h = n // 2
    bf = jnp.bfloat16
    st_ab[0] = jnp.concatenate([src[0, :, :h] + src[0, :, h:], src[1, :, :h] + src[1, :, h:]], axis=1).astype(bf)
    st_ab[1] = jnp.concatenate([src[0, :, :h] - src[0, :, h:], src[1, :, :h] - src[1, :, h:]], axis=1).astype(bf)


HBM = pl.BlockSpec(memory_space=pltpu.HBM)
VM = pl.BlockSpec(memory_space=pltpu.VMEM)
SM = pl.BlockSpec(memory_space=pltpu.SMEM)
F32, BF16 = jnp.float32, jnp.bfloat16


def params(mib):
    return pltpu.CompilerParams(vmem_limit_bytes=mib * 1024 * 1024)


def share(fronts, depth):
    d = lax.axis_index("depth")
    base, extra = fronts // depth, fronts % depth
    return d, base + jnp.where(d < extra, 1, 0), d * base + jnp.minimum(d, extra)


def first_levels(dims, om_h, slow_h, T_h, K2_h, win_h, src, rcv, st, own_out, slow, T, K2, win, om_out,
                 om, raw, P, c, D, sem_in, sem_t):
    n, slots, L, fronts, depth = dims
    d, nf, f0 = share(fronts, depth)

    def moves(j):
        fr = jnp.minimum(f0 + j, fronts - 1)
        return (
            pltpu.make_async_copy(src.at[fr], raw.at[j, 0], sem_in.at[j, 0]),
            pltpu.make_async_copy(rcv.at[fr], raw.at[j, 1], sem_in.at[j, 1]),
        )

    small = [
        pltpu.make_async_copy(a, b, sem_t.at[i])
        for i, (a, b) in enumerate(((om_h, om), (slow_h, slow), (T_h, T), (K2_h, K2), (win_h, win)))
    ]

    def each(j, act):
        if j < fronts // depth:
            act()
        else:
            pl.when(j < nf)(act)

    def begin(j):
        for m in moves(j):
            m.start()

    def ready(j):
        for f, m in enumerate(moves(j)):
            m.wait()
            prep(n, raw.at[j, f], st.at[j, f])

    each(0, lambda: begin(0))
    for m in small:
        m.start()
    for j in range(1, slots):
        each(j, functools.partial(begin, j))
    for j in range(slots):
        each(j, functools.partial(ready, j))
    for m in small:
        m.wait()
    for f in range(fronts):
        om_out[0, f] = om[0, f]

    def level(z, _):
        level_math(n, [om[0, f0 + j] for j in range(slots)], slow.at[z], T, K2, win, st, own_out.at[z], P, c, D)
        return 0

    lax.fori_loop(0, jnp.where(d == 0, L, 0), level, 0)


def other_levels(dims, om, st_in, slow, got, own_in, T, K2, win, keep_own, send_own, keep_oth, send_oth, st,
                 s_now, part, P, c, D):
    n, slots, L, fronts, depth, freq = dims
    d, nf, f0 = share(fronts, depth)
    fq = lax.axis_index("freq")
    lo = jnp.where(d == 0, L, 0)
    w = n // freq

    def split(ref, keep, sends):
        for a in range(freq):
            @pl.when(fq == a)
            def _():
                keep[...] = ref[:, a * w:(a + 1) * w]
                for r in range(1, freq):
                    b = (a + r) % freq
                    sends.at[r - 1][...] = ref[:, b * w:(b + 1) * w].astype(BF16)

    @pl.when(lo > 0)
    def _():
        for z in range(L):
            split(own_in.at[z], keep_own.at[z], send_own.at[:, z])

    def level(z, _):
        owner = z // L
        zl = z - owner * L
        back = lax.rem(d - owner + depth, depth)

        @pl.when(back == 0)
        def _():
            s_now[...] = slow[zl]

        @pl.when(back > 0)
        def _():
            s_now[...] = got[jnp.maximum(back - 1, 0), zl].astype(F32) + 1.0

        for count in sorted({slots, fronts // depth} - {0}):
            @pl.when(nf == count)
            def _():
                level_math(n, [om[0, f0 + j] for j in range(count)], s_now, T, K2, win, st, part, P, c, D)

        if fronts < depth:
            @pl.when(nf == 0)
            def _():
                part[...] = jnp.zeros((n, n), F32)

        @pl.when(back == 0)
        def _():
            split(part, keep_own.at[zl], send_own.at[:, zl])

        @pl.when(back > 0)
        def _():
            r = jnp.maximum(depth - back - 1, 0)
            split(part, keep_oth.at[r, zl], send_oth.at[:, r, zl])

        return 0

    lax.fori_loop(lo, depth * L, level, 0)


def place(dims, start, own, got, out, padded):
    n, L, shots, more = dims
    w = own.shape[-1]
    survey = shots * TILE
    me, begin = lax.axis_index("shot"), start[0]
    padded[:, :survey] = jnp.zeros((L, survey, w), F32)
    padded[:, survey + n:] = jnp.zeros((L, survey, w), F32)
    for z in range(L):
        total = own[z]
        for r in range(more):
            total = total + got[r, z].astype(F32)
        padded[z, survey:survey + n] = total
    for r in range(shots):
        owner = lax.rem(me + r, shots)
        offset = jnp.clip(owner * TILE - begin + survey, 0, n + survey)
        for z in range(L):
            out[r, z] = padded[z, pl.ds(offset, TILE), :].astype(BF16)


def gather(dims, *refs):
    L, shots = dims
    out = refs[-1]
    for z in range(L):
        total = refs[0][z].astype(F32)
        for r in range(1, shots):
            total = total + refs[r][z].astype(F32)
        out[:, z, :] = total


def pinned(array):
    return pltpu.with_memory_space_constraint(array, pltpu.HBM)


def shift(array, axis, by):
    size = lax.axis_size(axis)
    return lax.ppermute(array, axis, [(i, (i + by) % size) for i in range(size)])


def local(source, receiver, slowness, omegas, shot_start):
    n = source.shape[-1]
    h = n // 2
    fronts, L = source.shape[1], slowness.shape[1]
    depth, freq, shots = lax.axis_size("depth"), lax.axis_size("freq"), lax.axis_size("shot")
    T, K2, win = make_tables(n)
    slots = -(-fronts // depth)
    w = n // freq
    S = jax.ShapeDtypeStruct
    V = pltpu.VMEM
    slow = slowness[0]

    sent = (slow - 1.0).astype(BF16)
    got = jnp.stack([shift(sent, "depth", r) for r in range(1, depth)])

    math_scratch = [V((slots, 2, h + 8, n), F32), V((slots, 2, n, n), F32), V((3, n, n), F32)]
    state, own_a, slow_v, T_v, K2_v, win_v, om = pl.pallas_call(
        functools.partial(first_levels, (n, slots, L, fronts, depth)),
        out_shape=(S((slots, 2, 2, n, n), BF16), S((L, n, n), F32), S((L, n, n), F32), S((4, 2, n, n), BF16),
                   S((h + 8, h), F32), S((n, n), F32), S((1, fronts), F32)),
        in_specs=[HBM] * 7,
        out_specs=(VM, VM, VM, VM, VM, VM, SM),
        scratch_shapes=[pltpu.SMEM((1, fronts), F32), V((slots, 2, 2, n, n), F32)] + math_scratch
        + [pltpu.SemaphoreType.DMA((slots, 2)), pltpu.SemaphoreType.DMA((5,))],
        compiler_params=params(40),
        cost_estimate=pl.CostEstimate(flops=8 * 10**9, bytes_accessed=10**7, transcendentals=10**6),
        name="first_levels",
    )(*map(pinned, (omegas, slow, jnp.asarray(T), jnp.asarray(K2), jnp.asarray(win), source[0], receiver[0])))

    keep_own, send_own, keep_oth, send_oth, _ = pl.pallas_call(
        functools.partial(other_levels, (n, slots, L, fronts, depth, freq)),
        out_shape=(S((L, n, w), F32), S((freq - 1, L, n, w), BF16),
                   S((depth - 1, L, n, w), F32), S((freq - 1, depth - 1, L, n, w), BF16),
                   S(state.shape, state.dtype)),
        in_specs=[SM, VM, VM, VM, VM, VM, VM, VM],
        out_specs=(VM, VM, VM, VM, VM),
        input_output_aliases={1: 4},
        scratch_shapes=[V((n, n), F32), V((n, n), F32)] + math_scratch,
        compiler_params=params(32),
        cost_estimate=pl.CostEstimate(flops=8 * 10**9, bytes_accessed=10**7, transcendentals=10**6),
        name="other_levels",
    )(om, state, slow_v, got, own_a, T_v, K2_v, win_v)

    own, oth = keep_own, keep_oth
    for r in range(1, freq):
        oth = oth + shift(send_oth[r - 1], "freq", r).astype(F32)
    for r in range(1, freq):
        own = own + shift(send_own[r - 1], "freq", r).astype(F32)
    oth = oth.astype(BF16)
    own, start = lax.optimization_barrier((own, shot_start))
    arrived = jnp.stack([shift(oth[r - 1], "depth", r) for r in range(1, depth)])

    blocks = pl.pallas_call(
        functools.partial(place, (n, L, shots, depth - 1)),
        out_shape=S((shots, L, TILE, w), BF16),
        in_specs=[SM, VM, VM],
        out_specs=VM,
        scratch_shapes=[V((L, 2 * shots * TILE + n, w), F32)],
        compiler_params=params(32),
        name="place",
    )(start, own, arrived)
    pieces = [blocks[0]] + [shift(blocks[r], "shot", r) for r in range(1, shots)]
    return pl.pallas_call(
        functools.partial(gather, (L, shots)),
        out_shape=S((TILE, L, w), F32),
        in_specs=[VM] * shots,
        out_specs=VM,
        compiler_params=params(16),
        name="gather",
    )(*pieces)


def solution(mesh):
    return jax.shard_map(
        local,
        mesh=mesh,
        in_specs=(
            P_(("groups", "shot"), "freq", None, None, None),
            P_(("groups", "shot"), "freq", None, None, None),
            P_(("groups", "shot"), "depth", None, None),
            P_(("groups", "shot"), "freq"),
            P_(("groups", "shot")),
        ),
        out_specs=P_(("groups", "shot"), "depth", "freq"),
        check_vma=False,
    )
```

```python
import functools

import jax
import jax.numpy as jnp
import ml_dtypes
import numpy as np
from jax import lax
from jax.experimental import pallas as pl
from jax.experimental.pallas import tpu as pltpu
from jax.sharding import PartitionSpec as P_

TILE = 128

def _fit(f, hi, deg):
    k = np.arange(400)
    x = (np.cos(np.pi * (k + 0.5) / 400) + 1) / 2 * hi
    c = np.polynomial.chebyshev.Chebyshev.fit(x, f(x), deg, domain=[0, hi])
    return [float(v) for v in c.convert(kind=np.polynomial.Polynomial).coef]
def _cosr(a): return np.cos(np.sqrt(a))
def _sinr(a): return np.sinc(np.sqrt(a) / np.pi)
PC = _fit(_cosr, 12.5, 6); PS = _fit(_sinr, 12.5, 5)
CC = _fit(lambda a: (_cosr(a) - 1) / a, 4.1, 4); CS = _fit(_sinr, 4.1, 4)

def horner(co, x):
    r = co[-1] * x + co[-2]
    for c in co[-3::-1]:
        r = r * x + c
    return r

def make_tables(n):
    h, g = n // 2, n // 4
    idx = np.arange(n)
    ang = 2 * np.pi / n * (np.outer(idx, idx) % n)
    C = np.cos(ang).astype(ml_dtypes.bfloat16).astype(np.float32)
    S = np.sin(ang).astype(ml_dtypes.bfloat16).astype(np.float32)
    i = np.arange(g)
    ev = np.concatenate([2 * i, np.where(i == 0, h, n - 2 * i)])
    od = np.concatenate([2 * i + 1, n - 2 * i - 1])
    out = []
    for k in (ev, od):
        c, s = C[:h][:, k], S[:h][:, k]
        F = np.block([[c, -s], [s, c]])
        L = np.block([[c.T, s.T], [-s.T, c.T]])
        out.append((F, L, F / 1.0, L))
    T = []
    for p in (0, 1):
        k = (ev, od)[p]
        c, s = C[:h][:, k], S[:h][:, k]
        T.append(np.stack([np.block([[c, -s], [s, c]]), np.block([[c.T, s.T], [-s.T, c.T]]),
                           np.block([[c, -s], [s, c]]) / n, np.block([[c.T, s.T], [-s.T, c.T]]) / n]))
    T = np.stack(T, axis=1).astype(ml_dtypes.bfloat16)
    w = ((idx + h) % n - h).astype(np.float32)
    kk = (np.float32(2 * np.pi) / np.float32(n) * w).astype(np.float32)
    k2 = (kk * kk).astype(np.float32)
    base = np.concatenate([k2[2 * i], k2[2 * i + 1]])
    rows = np.concatenate([base, k2[h:h + 1]])
    K2 = np.zeros((h + 8, h), np.float32)
    K2[:h + 1] = rows[:, None] + base[None, :]
    K2[h + 1] = k2[h] + k2[h]
    ed = np.minimum(np.minimum(idx, n - 1 - idx) + 1, n // 16).astype(np.float32) / np.float32(n // 16)
    win = (ed[:, None] * ed[None, :]).astype(np.float32)
    return T, K2, win

def level_prep(n, s, win, D):
    s0 = jnp.sum(s[...]) * (1.0 / (n * n))
    d = s[...] - s0
    x = d * d
    D[0] = x
    D[1] = d * win[...]
    D[2] = x * win[...]
    return s0

def propagator(n, w2, K2, P):
    h, g = n // 2, n // 4
    a = w2 - K2[...]
    pos = a >= 0.0
    r = jnp.sqrt(jnp.abs(a))
    vals = (jnp.where(pos, horner(PC, a), jnp.exp(-r)), jnp.where(pos, r * horner(PS, a), 0.0))
    lane = lax.broadcasted_iota(jnp.int32, (8, h), 1)
    low, mid = lane < g, lane == g
    row0 = lax.broadcasted_iota(jnp.int32, (8, n), 0) == 0
    for comp in (0, 1):
        v = vals[comp]
        col = jnp.broadcast_to(v[h:h + 1], (h, h)).T
        for t in range(h // 8 + 1):
            p = v[8 * t:8 * t + 8]
            q = pltpu.roll(p, g, 1)
            cc = col[8 * t:8 * t + 8] if t < h // 8 else jnp.broadcast_to(v[h + 1:h + 2, :], (8, h))
            e = jnp.where(mid, cc, jnp.where(low, p, q))
            o = jnp.where(low, q, p)
            if t < g // 8:
                P[comp, 8 * t:8 * t + 8, :h] = e
                P[comp, 8 * t:8 * t + 8, h:] = o
                if t == 0:
                    e0, o0 = e, o
            elif t < h // 8:
                P[comp, 8 * t + 8:8 * t + 16, :h] = e
                P[comp, 8 * t + 8:8 * t + 16, h:] = o
            else:
                P[comp, g:g + 8, :h] = jnp.where(row0[:, :h], e, e0)
                P[comp, g:g + 8, h:] = jnp.where(row0[:, :h], o, o0)

def p_rows(n, P, comp, par):
    h, g = n // 2, n // 4
    if par == 0:
        return jnp.concatenate([P[comp, 0:g], P[comp, g:g + 8], P[comp, 8:g]], axis=0)
    o = P[comp, g + 8:h + 8]
    return jnp.concatenate([o, o], axis=0)

def corr(om, win, D, c):
    cc, cs, f = [], [], om
    for k in range(len(CC)):
        cs.append(CS[k] * f)
        f = f * om
        cc.append(CC[k] * f)
        f = f * om
    x = D[0]
    c[0] = win[...] + D[2] * horner(cc, x)
    c[1] = D[1] * horner(cs, x)

def front_math(n, om, s0, T, K2, win, st, P, c, D):
    h = n // 2
    f32, bf = jnp.float32, jnp.bfloat16
    dot = functools.partial(jnp.dot, preferred_element_type=f32)
    w2 = om * s0; w2 = w2 * w2
    FL = ((0, -1.0), (1, 1.0))
    add, sub = (lambda a, b: a + b), (lambda a, b: a - b)
    def stack2(X, Y, op):
        re = jnp.concatenate([op(X[:h, :h], X[h:, :h]), op(Y[:h, :h], Y[h:, :h])], axis=1)
        im = jnp.concatenate([op(X[:h, h:], X[h:, h:]), op(Y[:h, h:], Y[h:, h:])], axis=1)
        return jnp.concatenate([re, im], axis=0).astype(bf)
    R = []
    for f, sg in FL:
        Ve = dot(st[f, 0], T[0, 0]); Vo = dot(st[f, 1], T[0, 1])
        R.append((stack2(Ve, Vo, add), stack2(Ve, Vo, sub)))
    propagator(n, w2, K2, P)
    W2 = []
    for f, sg in FL:
        out = []
        for p in (0, 1):
            W = dot(T[1, p], R[f][p])
            wr, wi = W[:h], W[h:]
            pr, pi = p_rows(n, P, 0, p), p_rows(n, P, 1, p)
            if sg > 0:
                out.append(jnp.concatenate([wr * pr - wi * pi, wr * pi + wi * pr], axis=0).astype(bf))
            else:
                out.append(jnp.concatenate([wr * pr + wi * pi, wi * pr - wr * pi], axis=0).astype(bf))
        W2.append(out)
    corr(om, win, D, c)
    YY = []
    for f, sg in FL:
        E = dot(T[2, 0], W2[f][0]); O = dot(T[2, 1], W2[f][1])
        U, Dn = E + O, E - O
        out = []
        for p in (0, 1):
            sl = slice(p * h, (p + 1) * h)
            out.append(jnp.concatenate([jnp.concatenate([U[:h, sl], U[h:, sl]], axis=1),
                                        jnp.concatenate([Dn[:h, sl], Dn[h:, sl]], axis=1)], axis=0).astype(bf))
        YY.append(out)
    res = []
    for f, sg in FL:
        Q0, Q1 = dot(YY[f][0], T[3, 0]), dot(YY[f][1], T[3, 1])
        X, Z = Q0 + Q1, Q0 - Q1
        halves = []
        for hf, q in ((0, X), (1, Z)):
            qr, qi = q[:, :h], q[:, h:]
            cr, ci = c[0, :, hf * h:(hf + 1) * h], c[1, :, hf * h:(hf + 1) * h]
            if sg > 0:
                halves.append((qr * cr - qi * ci, qr * ci + qi * cr))
            else:
                halves.append((qr * cr + qi * ci, qi * cr - qr * ci))
        (r0, i0), (r1, i1) = halves
        st[f, 0] = jnp.concatenate([r0 + r1, i0 + i1], axis=1).astype(bf)
        st[f, 1] = jnp.concatenate([r0 - r1, i0 - i1], axis=1).astype(bf)
        res.append(halves)
    terms = []
    for hf in (0, 1):
        (ur, ui), (wr, wi) = res[0][hf], res[1][hf]
        terms.append(ur * wr + ui * wi)
    return terms


def level_math(n, oms, s, T, K2, win, st, part, P, c, D):
    h = n // 2
    s0 = level_prep(n, s, win, D)
    terms = [front_math(n, om, s0, T, K2, win, st.at[j], P.at[j], c.at[j], D) for j, om in enumerate(oms)]
    for hf in (0, 1):
        part[:, hf * h:(hf + 1) * h] = functools.reduce(lambda a, b: a + b, [t[hf] for t in terms])


def prep(n, src, st_ab):
    h = n // 2
    bf = jnp.bfloat16
    st_ab[0] = jnp.concatenate([src[0, :, :h] + src[0, :, h:], src[1, :, :h] + src[1, :, h:]], axis=1).astype(bf)
    st_ab[1] = jnp.concatenate([src[0, :, :h] - src[0, :, h:], src[1, :, :h] - src[1, :, h:]], axis=1).astype(bf)


HBM = pl.BlockSpec(memory_space=pltpu.HBM)
VM = pl.BlockSpec(memory_space=pltpu.VMEM)
SM = pl.BlockSpec(memory_space=pltpu.SMEM)
F32, BF16 = jnp.float32, jnp.bfloat16


def params(mib):
    return pltpu.CompilerParams(vmem_limit_bytes=mib * 1024 * 1024)


class Plan:
    def __init__(self, n, L, fronts, depth, freq):
        self.n, self.L, self.fronts, self.depth, self.freq = n, L, fronts, depth, freq
        self.levels = depth * L
        self.base, self.extra = fronts // depth, fronts % depth
        self.slots = self.base + (1 if self.extra else 0)

    def share(self):
        d = lax.axis_index("depth")
        late = jnp.maximum(d - (self.depth - self.extra), 0)
        more = jnp.where(d >= self.depth - self.extra, 1, 0)
        return d, self.base + more, d * self.base + late

    def span(self, step, d):
        L, S = self.L, self.levels
        first, last = d == 0, d == self.depth - 1
        if step == 0:
            return 0, jnp.where(first, L, 0)
        if step == 1:
            return jnp.where(first, L, 0), jnp.where(first, L + 1, 1)
        if step == 2:
            return jnp.where(first, L + 1, 1), jnp.where(last, S - L, S)
        if step == 3:
            return S - L, jnp.where(last, S - 1, S - L)
        return S - 1, jnp.where(last, S, S - 1)

    def counts(self, step):
        of = [self.base + (1 if d >= self.depth - self.extra else 0) for d in range(self.depth)]
        of = of[:1] if step == 0 else of[-1:] if step >= 3 else of
        return sorted(set(of))


def run_levels(plan, step, om, slow, got, T, K2, win, st, keep_own, send_own, keep_oth, send_oth, s_now, part, P, c, D):
    n, L, depth, freq = plan.n, plan.L, plan.depth, plan.freq
    d, nf, f0 = plan.share()
    fq = lax.axis_index("freq")
    w = n // freq

    def split(keep, sends):
        for a in range(freq):
            @pl.when(fq == a)
            def _():
                keep[...] = part[:, a * w:(a + 1) * w]
                for r in range(1, freq):
                    b = (a + r) % freq
                    sends.at[r - 1][...] = part[:, b * w:(b + 1) * w].astype(BF16)

    def level(z, _):
        owner = z // L
        zl = z - owner * L
        back = lax.rem(d - owner + depth, depth)

        @pl.when(back == 0)
        def _():
            s_now[...] = slow[zl]

        if got:
            r = jnp.maximum(back - 1, 0)

            @pl.when(jnp.logical_and(back > 0, zl == 0))
            def _():
                s_now[...] = got[0][r].astype(F32) + 1.0

        if len(got) > 1:
            @pl.when(jnp.logical_and(back > 0, zl > 0))
            def _():
                s_now[...] = got[1][r, jnp.maximum(zl - 1, 0)].astype(F32) + 1.0

        for count in plan.counts(step):
            def go():
                if count == 0:
                    part[...] = jnp.zeros((n, n), F32)
                else:
                    oms = [om[0, f0 + j] for j in range(count)]
                    level_math(n, oms, s_now, T, K2, win, st, part, P, c, D)
            if len(plan.counts(step)) == 1:
                go()
            else:
                pl.when(nf == count)(go)

        @pl.when(back == 0)
        def _():
            split(keep_own.at[zl], send_own.at[:, zl])

        if keep_oth is not None:
            @pl.when(back > 0)
            def _():
                to = jnp.maximum(depth - back - 1, 0)
                split(keep_oth.at[to, zl], send_oth.at[:, to, zl])

        return 0

    lo, hi = plan.span(step, d)
    lax.fori_loop(lo, hi, level, 0)


def enter(plan, om_h, slow_h, T_h, K2_h, win_h, src, rcv, om_out, slow, T, K2, win, st, keep_own, send_own, keep_oth,
          send_oth, om, raw, *rest):
    n, fronts = plan.n, plan.fronts
    sem_in, sem_t = rest[-2:]
    d, nf, f0 = plan.share()

    def moves(j):
        fr = jnp.minimum(f0 + j, fronts - 1)
        return (
            pltpu.make_async_copy(src.at[fr], raw.at[j, 0], sem_in.at[j, 0]),
            pltpu.make_async_copy(rcv.at[fr], raw.at[j, 1], sem_in.at[j, 1]),
        )

    small = [
        pltpu.make_async_copy(a, b, sem_t.at[i])
        for i, (a, b) in enumerate(((om_h, om), (slow_h, slow), (T_h, T), (K2_h, K2), (win_h, win)))
    ]

    def each(j, act):
        if j < plan.base:
            act()
        else:
            pl.when(j < nf)(act)

    def begin(j):
        for m in moves(j):
            m.start()

    def ready(j):
        for f, m in enumerate(moves(j)):
            m.wait()
            prep(n, raw.at[j, f], st.at[j, f])

    each(0, lambda: begin(0))
    for m in small:
        m.start()
    for j in range(1, plan.slots):
        each(j, functools.partial(begin, j))
    for j in range(plan.slots):
        each(j, functools.partial(ready, j))
    for m in small:
        m.wait()
    for f in range(fronts):
        om_out[0, f] = om[0, f]
    run_levels(plan, 0, om, slow, (), T, K2, win, st, keep_own, send_own, keep_oth, send_oth, *rest[:-2])


def carry_on(plan, step, n_got, n_out, n_after, *refs):
    om, slow, T, K2, win = refs[:5]
    got = refs[5:5 + n_got]
    here = 5 + n_got + n_out + n_after
    outs = refs[here:here + n_out]
    work = refs[here + n_out:]
    if n_out == 3:
        outs = (*outs, None, None)
    run_levels(plan, step, om, slow, got, T, K2, win, *outs, *work)


def place(dims, start, own, got, out, padded):
    n, L, shots, more = dims
    w = own.shape[-1]
    survey = shots * TILE
    me, begin = lax.axis_index("shot"), start[0]
    padded[:, :survey] = jnp.zeros((L, survey, w), F32)
    padded[:, survey + n:] = jnp.zeros((L, survey, w), F32)
    for z in range(L):
        total = own[z]
        for r in range(more):
            total = total + got[r, z].astype(F32)
        padded[z, survey:survey + n] = total
    for r in range(shots):
        owner = lax.rem(me + r, shots)
        offset = jnp.clip(owner * TILE - begin + survey, 0, n + survey)
        for z in range(L):
            out[r, z] = padded[z, pl.ds(offset, TILE), :].astype(BF16)


def gather(dims, *refs):
    L, shots = dims
    out = refs[-1]
    for z in range(L):
        total = refs[0][z].astype(F32)
        for r in range(1, shots):
            total = total + refs[r][z].astype(F32)
        out[:, z, :] = total


def pinned(array):
    return pltpu.with_memory_space_constraint(array, pltpu.HBM)


def shift(array, axis, by):
    size = lax.axis_size(axis)
    return lax.ppermute(array, axis, [(i, (i + by) % size) for i in range(size)])


def local(source, receiver, slowness, omegas, shot_start):
    n = source.shape[-1]
    h = n // 2
    fronts, L = source.shape[1], slowness.shape[1]
    depth, freq, shots = lax.axis_size("depth"), lax.axis_size("freq"), lax.axis_size("shot")
    plan = Plan(n, L, fronts, depth, freq)
    T, K2, win = make_tables(n)
    slots, w = plan.slots, n // freq
    S, V = jax.ShapeDtypeStruct, pltpu.VMEM
    slow = slowness[0]

    def known(part):
        sent = (part - 1.0).astype(BF16)
        return jnp.stack([shift(sent, "depth", r) for r in range(1, depth)])

    got = [known(slow[0])]
    if L > 1:
        got.append(known(slow[1:]))

    work = [V((n, n), F32), V((n, n), F32), V((slots, 2, h + 8, n), F32), V((slots, 2, n, n), F32), V((3, n, n), F32)]
    share_own = [S((L, n, w), F32), S((freq - 1, L, n, w), BF16)]
    share_oth = [S((depth - 1, L, n, w), F32), S((freq - 1, depth - 1, L, n, w), BF16)]
    cost = pl.CostEstimate(flops=4 * 10**9, bytes_accessed=10**7, transcendentals=10**6)
    tables = [S((1, fronts), F32), S((L, n, n), F32), S((4, 2, n, n), BF16), S((h + 8, h), F32), S((n, n), F32)]
    state = [S((slots, 2, 2, n, n), BF16), *share_own, *share_oth]
    done = pl.pallas_call(
        functools.partial(enter, plan),
        out_shape=(*tables, *state),
        in_specs=[HBM] * 7,
        out_specs=(SM, *[VM] * 9),
        scratch_shapes=[pltpu.SMEM((1, fronts), F32), V((slots, 2, 2, n, n), F32), *work,
                        pltpu.SemaphoreType.DMA((slots, 2)), pltpu.SemaphoreType.DMA((5,))],
        compiler_params=params(40),
        cost_estimate=cost,
        name="enter",
    )(*map(pinned, (omegas, slow, jnp.asarray(T), jnp.asarray(K2), jnp.asarray(win), source[0], receiver[0])))
    fixed, moving = done[:5], done[5:]

    def carry(step, got, moving, after=()):
        m = len(moving)
        return pl.pallas_call(
            functools.partial(carry_on, plan, step, len(got), m, len(after)),
            out_shape=tuple(S(a.shape, a.dtype) for a in moving),
            in_specs=[SM, *[VM] * (4 + len(got) + m + len(after))],
            out_specs=(VM,) * m,
            input_output_aliases={5 + len(got) + i: i for i in range(m)},
            scratch_shapes=work,
            compiler_params=params(40),
            cost_estimate=cost,
            name="levels_" + str(step),
        )(*fixed, *got, *moving, *after)

    moving = carry(1, got[:1], moving)
    *moving, keep_oth, send_oth = carry(2, got, moving)
    oth = keep_oth
    for r in range(1, freq):
        oth = oth + shift(send_oth[r - 1], "freq", r).astype(F32)
    oth = oth.astype(BF16)
    moving = carry(3, (), moving)
    arrived = jnp.stack([shift(oth[r - 1], "depth", r) for r in range(1, depth)])
    _, own, send_own = carry(4, (), moving, after=[oth])
    for r in range(1, freq):
        own = own + shift(send_own[r - 1], "freq", r).astype(F32)
    start = jnp.maximum(shot_start, 0)

    blocks = pl.pallas_call(
        functools.partial(place, (n, L, shots, depth - 1)),
        out_shape=S((shots, L, TILE, w), BF16),
        in_specs=[SM, VM, VM],
        out_specs=VM,
        scratch_shapes=[V((L, 2 * shots * TILE + n, w), F32)],
        compiler_params=params(32),
        name="place",
    )(start, own, arrived)
    pieces = [blocks[0]] + [shift(blocks[r], "shot", r) for r in range(1, shots)]
    return pl.pallas_call(
        functools.partial(gather, (L, shots)),
        out_shape=S((TILE, L, w), F32),
        in_specs=[VM] * shots,
        out_specs=VM,
        compiler_params=params(16),
        name="gather",
    )(*pieces)


def solution(mesh):
    return jax.shard_map(
        local,
        mesh=mesh,
        in_specs=(
            P_(("groups", "shot"), "freq", None, None, None),
            P_(("groups", "shot"), "freq", None, None, None),
            P_(("groups", "shot"), "depth", None, None),
            P_(("groups", "shot"), "freq"),
            P_(("groups", "shot")),
        ),
        out_specs=P_(("groups", "shot"), "depth", "freq"),
        check_vma=False,
    )
```
